128 devices in a mesh: gx: 16 (over y, x_hi, core), gy: 8 (over x_lo, z).
Axes of the slice: x: 4 (x_hi: 2, x_lo: 2; x = x_hi * 2 + x_lo), y: 4, z: 4, core: 2. Of those that a mesh axis runs over, the one named last changes fastest.
Arguments:
- mixing: float32 [3, 8, 128, 1024], P(None, None, 'gx', 'gy'), may hold values from 0.02 to 0.5
- forcing: float32 [2, 8, 128, 1024], P(None, None, 'gx', 'gy'), may hold values from -6 to 6
- labels: int32 [8, 128, 1024], P(None, 'gx', 'gy'), may hold values from 0 to 2
- colours: int32 [16, 8], P('gx', 'gy'), may hold values from 0 to 5
- coarse_basis: float32 [2, 8, 128, 1024], P(None, None, 'gx', 'gy'), may hold values from 0.5 to 2
- coarse_inverse: float32 [16, 8, 2, 256], P('gx', 'gy'), may hold values from -4 to 4
Outputs:
- concentration: float32 [2, 8, 128, 1024], P(None, None, 'gx', 'gy')
- coarse_coeff: float32 [16, 8, 2], P('gx', 'gy')
The draws below stay inside these ranges and needn't reach their ends.
All inputs are finite; a program needn't handle non-finite values.
Results may differ from the reference program's by a relative error of at most 0.0003.
Values sent between devices are 32-bit elements; how exact they have to be, the bound alone decides.
No kernel may reach another device: no remote copies, remote signals or barrier semaphores. Data moves between devices by JAX's collectives and lax.ppermute only.
A program may use at most 64 MiB of HBM per device.

```python
import math
import jax
import jax.numpy as jnp
from jax import lax

CX = 8
CY = 128
NZ = 8
MARGIN = 4
SWEEPS = 20
ROUNDS = 6
SUBS = 128
NX = 128
NY = 1024
N_GX = 16
N_GY = 8


def plant(drawn, rng, least, top_value):
    shape = drawn.shape
    index_at = [jax.random.randint(jax.random.fold_in(rng, axis), (), 0, shape[axis]) for axis in range(len(shape))]
    drawn = drawn.at[tuple(index_at)].set(least)
    longest = shape.index(max(shape))
    index_at[longest] = (index_at[longest] + 1) % shape[longest]
    return drawn.at[tuple(index_at)].set(top_value)


def levels(stream_key, shape, pieces, least, top_value):
    loudness = 1.0
    for axis_at, blocks in pieces:
        steps = jax.random.uniform(jax.random.fold_in(jax.random.fold_in(stream_key, 6), axis_at), (blocks,), jnp.float32, least / len(pieces), top_value / len(pieces))
        loudness = loudness * jnp.repeat(jnp.exp(steps), shape[axis_at] // blocks).reshape((-1,) + (1,) * (len(shape) - 1 - axis_at))
    return loudness


def scatter_about(rng, shape, width, limit, pieces=(), held_as=jnp.bfloat16):
    level = levels(rng, shape, pieces, -0.22, 0.18) if pieces else 1.0
    drawn = jax.random.normal(rng, shape, jnp.float32) * width * level
    return jnp.minimum(jnp.maximum(drawn, -limit), limit).astype(held_as)


def setup_inputs(seed: int = 0) -> dict:
    arg_keys = jax.random.split(jax.random.key(seed), 7)
    return {
        "mixing": jnp.clip(jnp.exp(math.log(0.5) - 3.218876 * jax.random.uniform(arg_keys[0], (3, NZ, NX, NY), jnp.float32) ** levels(arg_keys[0], (3, NZ, NX, NY), ((2, 16), (3, 8)), -0.2, 0.2)), 0.02, 0.5),
        "forcing": scatter_about(arg_keys[1], (2, NZ, NX, NY), 1.0, 6.0, ((2, 16), (3, 8)), jnp.float32),
        "labels": plant(jax.random.randint(arg_keys[2], (NZ, NX, NY), 0, 3), jax.random.fold_in(arg_keys[2], 1), 0, 2).astype(jnp.int32),
        "colours": plant(jax.random.randint(arg_keys[3], (N_GX, N_GY), 0, 6), jax.random.fold_in(arg_keys[3], 1), 0, 5).astype(jnp.int32),
        "coarse_basis": jnp.clip(jnp.exp(math.log(2.0) - 1.3862944 * jax.random.uniform(arg_keys[4], (2, NZ, NX, NY), jnp.float32) ** levels(arg_keys[4], (2, NZ, NX, NY), ((2, 16), (3, 8)), -0.2, 0.2)), 0.5, 2.0),
        "coarse_inverse": scatter_about(arg_keys[5], (N_GX, N_GY, 2, 2 * SUBS), 2 ** -0.5, 4.0, ((0, 16), (1, 8)), jnp.float32),
    }


ROBIN = 1.0
OMEGA = 0.8


def neighbour_op(padded, s11, s22, s12, diag):
    centre = padded[:, :, 1:-1, 1:-1]
    zpad = jnp.pad(centre, ((0, 0), (1, 1), (0, 0), (0, 0)))
    near = padded[:, :, 2:, 1:-1] + padded[:, :, :-2, 1:-1]
    near = near + padded[:, :, 1:-1, 2:] + padded[:, :, 1:-1, :-2]
    near = near + zpad[:, 2:] + zpad[:, :-2]
    first = s11 * centre[0] + s12 * centre[1] + diag * centre[0] - near[0]
    second = s12 * centre[0] + s22 * centre[1] + diag * centre[1] - near[1]
    return jnp.stack([first, second])


def margin_tables(first_x, first_y, ext_x, ext_y, total_x, total_y):
    index_x = jnp.arange(ext_x, dtype=jnp.int32)
    index_y = jnp.arange(ext_y, dtype=jnp.int32)
    cells_x = first_x - MARGIN + index_x
    cells_y = first_y - MARGIN + index_y
    in_x = (cells_x >= 0) & (cells_x < total_x)
    in_y = (cells_y >= 0) & (cells_y < total_y)
    inside = (in_x[:, None] & in_y[None, :]).astype(jnp.float32)
    rim_x = ((index_x == 0) & (cells_x - 1 >= 0)).astype(jnp.float32) + ((index_x == ext_x - 1) & (cells_x + 1 < total_x)).astype(jnp.float32)
    rim_y = ((index_y == 0) & (cells_y - 1 >= 0)).astype(jnp.float32) + ((index_y == ext_y - 1) & (cells_y + 1 < total_y)).astype(jnp.float32)
    count = rim_x[:, None] + rim_y[None, :]
    return inside, count


def local_solve(residual, s11, s22, s12, inside, count):
    diag = 6.0 + ROBIN * count
    scale = jnp.stack([s11 + diag, s22 + diag])
    correction = jnp.zeros_like(residual)
    for sweep in range(SWEEPS):
        padded = jnp.pad(correction, ((0, 0), (0, 0), (1, 1), (1, 1)))
        image = neighbour_op(padded, s11, s22, s12, diag)
        correction = (correction + OMEGA * (residual - image) / scale) * inside
    return correction


def couplings(mixing):
    return mixing[0], mixing[1], 0.25 * (mixing[2] - 0.125)


def reference(mixing, forcing, labels, colours, coarse_basis, coarse_inverse):
    s11, s22, s12 = couplings(mixing)
    onehot = jnp.stack([labels == 1, labels == 2]).astype(jnp.float32)
    rhs = onehot + forcing
    state = onehot
    mixing_pad = jnp.pad(mixing, ((0, 0), (0, 0), (MARGIN, MARGIN), (MARGIN, MARGIN)))
    ext_x = CX + 2 * MARGIN
    ext_y = CY + 2 * MARGIN
    for rnd in range(ROUNDS):
        padded = jnp.pad(state, ((0, 0), (0, 0), (1, 1), (1, 1)))
        residual = rhs - neighbour_op(padded, s11, s22, s12, 6.0)
        residual_pad = jnp.pad(residual, ((0, 0), (0, 0), (MARGIN, MARGIN), (MARGIN, MARGIN)))

        def solve_one(index):
            row = index // N_GY
            col = index % N_GY
            first_x = (row * CX).astype(jnp.int32)
            first_y = (col * CY).astype(jnp.int32)
            zero = jnp.zeros((), jnp.int32)
            local_res = lax.dynamic_slice(residual_pad, (zero, zero, first_x, first_y), (2, NZ, ext_x, ext_y))
            local_mix = lax.dynamic_slice(mixing_pad, (zero, zero, first_x, first_y), (3, NZ, ext_x, ext_y))
            inside, count = margin_tables(first_x, first_y, ext_x, ext_y, NX, NY)
            m11, m22, m12 = couplings(local_mix)
            correction = local_solve(local_res * inside, m11, m22, m12, inside, count)
            chosen = (colours[row, col] == rnd).astype(jnp.float32)
            return correction[:, :, MARGIN:MARGIN + CX, MARGIN:MARGIN + CY] * chosen

        blocks = lax.map(solve_one, jnp.arange(SUBS, dtype=jnp.int32))
        blocks = blocks.reshape(N_GX, N_GY, 2, NZ, CX, CY).transpose(2, 3, 0, 4, 1, 5).reshape(2, NZ, NX, NY)
        state = state + blocks
    padded = jnp.pad(state, ((0, 0), (0, 0), (1, 1), (1, 1)))
    residual = rhs - neighbour_op(padded, s11, s22, s12, 6.0)
    weighted = (coarse_basis * residual).reshape(2, NZ, N_GX, CX, N_GY, CY).sum(axis=(1, 3, 5)) / (NZ * CX * CY)
    values = weighted.transpose(1, 2, 0).reshape(2 * SUBS)
    coarse = jnp.einsum('abfc,c->abf', coarse_inverse, values, precision=lax.Precision.HIGHEST)
    lift = coarse.transpose(2, 0, 1)[:, None, :, None, :, None]
    shaped = state.reshape(2, NZ, N_GX, CX, N_GY, CY) + coarse_basis.reshape(2, NZ, N_GX, CX, N_GY, CY) * lift
    return shaped.reshape(2, NZ, NX, NY), coarse
```

```python
import jax
import jax.numpy as jnp
from jax import lax
from jax.experimental import pallas as pl
from jax.experimental.pallas import tpu as pltpu
from jax.sharding import PartitionSpec as P

SWEEPS = 20
OMEGA = 0.8
PAD = 8
WIN = (16, 13, 10, 7, 4)
KEEP = (104, 80, 56, 32, 8)
ROWS = 400
F32 = jnp.float32
NGX = 16
NGY = 8


def iota(shape, dim):
    return lax.broadcasted_iota(jnp.int32, shape, dim)


def roll(x, by, axis):
    by = by % x.shape[axis]
    return x if by == 0 else pltpu.roll(x, by, axis)


def lane_ids():
    lane = iota((8, 128), 1)
    return lane & 15, lane >> 4


def edge_columns(tiles):
    lane = iota((8, 128), 1)
    out = jnp.zeros((8, 128), F32)
    for n, tile in enumerate(tiles):
        out = jnp.where(lane == n, roll(tile, n, 1), out)
        out = jnp.where(lane == 16 + n, roll(tile, 17 + n, 1), out)
    return out


def pack_kernel(mix, forc, lab, basis, colour, out):
    for f in range(3):
        out[f * 8 : f * 8 + 8] = mix[f]
    for f in range(2):
        out[24 + f * 8 : 32 + f * 8] = forc[f]
    out[40:48] = lab[...].astype(F32)
    cols = edge_columns([basis[f, z] for f in range(2) for z in range(8)])
    lane = iota((8, 128), 1)
    out[48] = jnp.where(lane == 32, colour[0, 0].astype(F32), cols)


def rows_kernel(own, left, right, basis, up, down):
    for part, ref in enumerate((left, own, right)):
        lanes = slice(part * 128, part * 128 + 128)
        for a in range(6):
            for p in range(4):
                lo, hi = ref[a * 8 + 2 * p], ref[a * 8 + 2 * p + 1]
                sub = iota((8, 128), 0)
                up[a * 4 + p, :, lanes] = jnp.where(sub < 4, lo, roll(hi, 4, 0))
                down[a * 4 + p, :, lanes] = jnp.where(sub < 4, roll(lo, 4, 0), hi)
        for z in range(8):
            up[24, z : z + 1, lanes] = ref[40 + z, 4:5, :]
            down[24, z : z + 1, lanes] = ref[40 + z, 3:4, :]
            for f in range(2):
                if part == 1:
                    up[25 + f, z : z + 1, lanes] = basis[f, z, 0:1, :]
                    down[25 + f, z : z + 1, lanes] = basis[f, z, 7:8, :]
        if part != 1:
            up[25:27, :, lanes] = jnp.zeros((2, 8, 128), F32)
            down[25:27, :, lanes] = jnp.zeros((2, 8, 128), F32)


def window_rows(kind, tiles):
    if kind == 0:
        return PAD + 128 - 4
    if kind == 1:
        return PAD + 128 + 4 - 8 * tiles
    return PAD + 128 + 124


def prepare(kind, tiles, stat, u, uo, coef, i, j):
    row0 = window_rows(kind, tiles)
    xp, z = lane_ids()
    sub = iota((8, 128), 0)
    rim_x = ((xp == 0) | (xp == 15)).astype(F32)
    gx = i * 8 + xp - 4
    in_x = ((gx >= 0) & (gx < NGX * 8)).astype(F32)
    for t in range(tiles):
        at = pl.ds(row0 + t, 8, stride=tiles)
        s11, s22, s12 = stat[0, at, :], stat[1, at, :], stat[2, at, :]
        y = row0 - PAD - 128 + sub * tiles + t + j * 128
        inside = in_x * ((y >= 0) & (y < NGY * 128)).astype(F32)
        diag = 6.0 + rim_x
        if t == 0 and kind != 1:
            diag = diag + (sub == 0).astype(F32)
        if t == tiles - 1 and kind != 2:
            diag = diag + (sub == 7).astype(F32)
        vals = []
        for f in range(2):
            c = u[f, at, :]
            near = u[f, pl.ds(row0 + t - 1, 8, stride=tiles), :] + u[f, pl.ds(row0 + t + 1, 8, stride=tiles), :]
            out = uo[f, at, :]
            near = near + jnp.where(xp == 0, out, roll(c, 1, 1)) + jnp.where(xp == 15, out, roll(c, -1, 1))
            near = near + jnp.where(z == 0, 0.0, roll(c, 16, 1)) + jnp.where(z == 7, 0.0, roll(c, -16, 1))
            vals.append((c, near))
        for f, s in ((0, s11), (1, s22)):
            c, near = vals[f]
            r = stat[3 + f, at, :] - ((s + 6.0) * c + s12 * vals[1 - f][0] - near)
            w = OMEGA * inside / (s + diag)
            coef[f, t] = w
            coef[2 + f, t] = w * s12
            coef[4 + f, t] = w * r
            coef[6 + f, t] = w * r


def sweeps(kind, tiles, u, coef):
    row0 = window_rows(kind, tiles)
    xp, z = lane_ids()
    sub = iota((8, 128), 0)

    def body(_, carry):
        firsts, prevs = [], []
        for f in range(2):
            first = coef[6 + f, 0]
            firsts.append(jnp.where(sub == 7, 0.0, roll(first, -1, 0)))
            prevs.append(jnp.where(sub == 0, 0.0, roll(coef[6 + f, tiles - 1], 1, 0)))
        cur = [coef[6, 0], coef[7, 0]]
        for t in range(tiles):
            nxt = [coef[6, t + 1], coef[7, t + 1]] if t + 1 < tiles else firsts
            for f in range(2):
                c = cur[f]
                near = prevs[f] + nxt[f]
                near = near + (jnp.where(xp == 0, 0.0, roll(c, 1, 1)) + jnp.where(xp == 15, 0.0, roll(c, -1, 1)))
                near = near + (jnp.where(z == 0, 0.0, roll(c, 16, 1)) + jnp.where(z == 7, 0.0, roll(c, -16, 1)))
                new = (1.0 - OMEGA) * c + coef[4 + f, t] + (coef[f, t] * near - coef[2 + f, t] * cur[1 - f])
                coef[6 + f, t] = new
            prevs, cur = cur, nxt
        return carry

    lax.fori_loop(0, SWEEPS - 1, body, 0)
    own_x = (xp >= 4) & (xp < 12)
    for t in range(tiles):
        at = pl.ds(row0 + t, 8, stride=tiles)
        y = row0 - PAD - 128 + sub * tiles + t
        if kind == 0:
            here = own_x & (y >= 0) & (y < 128)
        elif kind == 1:
            here = own_x & (y < 0)
        else:
            here = own_x & (y >= 128)
        for f in range(2):
            u[f, at, :] = u[f, at, :] + jnp.where(here, coef[6 + f, t], 0.0)


def solve_round(rnd, stat, u, uo, meta, coefs, i, j):
    own = jnp.max(meta[0:8, :])
    left = jnp.max(meta[8:16, :])
    right = jnp.max(meta[16:24, :])
    jobs = [(0, 17, own, coefs[0])]
    if rnd < 5:
        jobs += [(1, WIN[rnd], left, coefs[1]), (2, WIN[rnd], right, coefs[2])]
    for kind, tiles, colour, coef in jobs:
        pl.when(colour == float(rnd))(lambda kind=kind, tiles=tiles, coef=coef: prepare(kind, tiles, stat, u, uo, coef, i, j))
    for kind, tiles, colour, coef in jobs:
        pl.when(colour == float(rnd))(lambda kind=kind, tiles=tiles, coef=coef: sweeps(kind, tiles, u, coef))


def emit(rnd, u, up, down):
    keep = KEEP[rnd]
    xp, _ = lane_ids()
    for q in range((128 + 2 * keep) // 8):
        src = pl.ds(PAD + 128 - keep + 8 * q, 8)
        a, b = u[0, src, :], u[1, src, :]
        up[pl.ds(8 * q, 8), :] = jnp.where(xp < 5, roll(a, -4, 1), roll(b, 1, 1))
        down[pl.ds(8 * q, 8), :] = jnp.where(xp < 5, roll(a, -7, 1), roll(b, -2, 1))


def absorb(rnd, u, uo, above, below, i):
    keep = KEEP[rnd]
    xp, _ = lane_ids()
    has_above = (i > 0).astype(F32)
    has_below = (i < NGX - 1).astype(F32)
    for q in range((128 + 2 * keep) // 8):
        at = pl.ds(PAD + 128 - keep + 8 * q, 8)
        a = above[pl.ds(8 * q, 8), :] * has_above
        b = below[pl.ds(8 * q, 8), :] * has_below
        u[0, at, :] = jnp.where(xp < 4, roll(a, -1, 1), jnp.where(xp >= 12, roll(b, 12, 1), u[0, at, :]))
        u[1, at, :] = jnp.where(xp < 4, roll(a, -6, 1), jnp.where(xp >= 12, roll(b, 7, 1), u[1, at, :]))
        uo[0, at, :] = jnp.where(xp == 0, a, roll(b, 11, 1))
        uo[1, at, :] = jnp.where(xp == 0, roll(a, -5, 1), roll(b, 6, 1))


def start_kernel(own, left, right, above, below, stat, u, meta, fin, up, down, buf, uo, c0, c1, c2):
    i = lax.axis_index("gx")
    j = lax.axis_index("gy")
    xp, _ = lane_ids()
    lane = iota((8, 128), 1)
    full_lane = iota((128, 128), 1)
    full_xp = full_lane & 15
    gx = i * 8 + full_xp - 4
    in_x = (gx >= 0) & (gx < NGX * 8)
    for n, ref in enumerate((own, left, right)):
        valid = ((j > 0) if n == 1 else (j < NGY - 1)) if n else (j >= 0)
        colour = jnp.where(lane == 32, jnp.where(valid, 1.0, 0.0) * (ref[48] + 1.0), 0.0) - 1.0
        meta[n * 8 : n * 8 + 8, :] = colour
    fin[0] = left[48] * (j > 0).astype(F32)
    fin[1] = right[48] * (j < NGY - 1).astype(F32)
    for f in range(2):
        fin[2 + f] = above[25 + f, :, 128:256] * (i > 0).astype(F32)
        fin[4 + f] = below[25 + f, :, 128:256] * (i < NGX - 1).astype(F32)
    for f in range(2):
        u[f, 0:PAD, :] = jnp.zeros((PAD, 128), F32)
        u[f, ROWS - PAD : ROWS, :] = jnp.zeros((PAD, 128), F32)
    for part, ref in enumerate((left, own, right)):
        lanes = slice(part * 128, part * 128 + 128)
        rows = slice(PAD + part * 128, PAD + part * 128 + 128)
        gy = (j - 1 + part) * 128
        in_y = (gy >= 0) & (gy < NGY * 128)

        def gather(a):
            slot = a % 2
            for p in range(4):
                for h in range(2):
                    z = 2 * p + h
                    buf[slot, z * 16 : z * 16 + 4, :] = above[a * 4 + p, 4 * h : 4 * h + 4, lanes]
                    buf[slot, z * 16 + 4 : z * 16 + 12, :] = ref[a * 8 + z]
                    buf[slot, z * 16 + 12 : z * 16 + 16, :] = below[a * 4 + p, 4 * h : 4 * h + 4, lanes]
            return buf[slot].T

        stat[0, rows, :] = gather(0)
        stat[1, rows, :] = gather(1)
        stat[2, rows, :] = 0.25 * (gather(2) - 0.125)
        force = [gather(3), gather(4)]
        label = gather(5)
        buf[0] = jnp.zeros((128, 128), F32)
        for z in range(8):
            buf[0, z * 16 : z * 16 + 1, :] = above[24, z : z + 1, lanes]
            buf[0, z * 16 + 15 : z * 16 + 16, :] = below[24, z : z + 1, lanes]
        outer = buf[0].T
        y_ok = in_y.astype(F32)
        out_ok = jnp.where(full_xp == 0, (i > 0).astype(F32), (i < NGX - 1).astype(F32)) * y_ok
        for f in range(2):
            hot = (label == f + 1.0).astype(F32) * (in_x.astype(F32) * y_ok)
            u[f, rows, :] = hot
            stat[3 + f, rows, :] = hot + force[f]
            uo[f, rows, :] = (outer == f + 1.0).astype(F32) * out_ok
    solve_round(0, stat, u, uo, meta, (c0, c1, c2), i, j)
    emit(0, u, up, down)


def middle_kernel(rnd, stat, u_in, meta, above, below, u, up, down, uo, c0, c1, c2):
    i = lax.axis_index("gx")
    j = lax.axis_index("gy")
    u[...] = u_in[...]
    absorb(rnd - 1, u, uo, above, below, i)
    solve_round(rnd, stat, u, uo, meta, (c0, c1, c2), i, j)
    emit(rnd, u, up, down)


def last_kernel(stat, u_in, meta, above, below, fin, mix, forc, lab, basis, nat, send, u, uo, c0):
    i = lax.axis_index("gx")
    j = lax.axis_index("gy")
    u[...] = u_in[...]
    absorb(4, u, uo, above, below, i)
    solve_round(5, stat, u, uo, meta, (c0,), i, j)
    sub = iota((8, 128), 0)
    lane = iota((8, 128), 1)
    tiles = []
    for f in range(2):
        flat = u[f, PAD + 128 : PAD + 256, :].T
        for z in range(8):
            tile = flat[z * 16 + 4 : z * 16 + 12, :]
            nat[f, z] = tile
            tiles.append(tile)
    cols = edge_columns(tiles)
    sums = [jnp.zeros((8, 128), F32) for _ in range(10)]
    left = cols * roll(fin[0], -16, 1)
    right = cols * roll(fin[1], 16, 1)
    for f in range(2):
        acc = jnp.zeros((8, 128), F32)
        for z in range(8):
            c, other = tiles[f * 8 + z], tiles[(1 - f) * 8 + z]
            near = jnp.where(sub == 0, 0.0, roll(c, 1, 0)) + jnp.where(sub == 7, 0.0, roll(c, -1, 0))
            near = near + jnp.where(lane == 0, 0.0, roll(c, 1, 1)) + jnp.where(lane == 127, 0.0, roll(c, -1, 1))
            if z > 0:
                near = near + tiles[f * 8 + z - 1]
            if z < 7:
                near = near + tiles[f * 8 + z + 1]
            s12 = 0.25 * (mix[2, z] - 0.125)
            rhs = (lab[z] == f + 1).astype(F32) + forc[f, z]
            acc = acc + basis[f, z] * (rhs - ((mix[f, z] + 6.0) * c + s12 * other - near))
        sums[f] = acc
        top = jnp.zeros((8, 128), F32)
        bot = jnp.zeros((8, 128), F32)
        for z in range(8):
            top = jnp.where(sub == z, jnp.broadcast_to(tiles[f * 8 + z][0:1, :], (8, 128)), top)
            bot = jnp.where(sub == z, jnp.broadcast_to(tiles[f * 8 + z][7:8, :], (8, 128)), bot)
        sums[2 + f] = top * fin[2 + f]
        sums[4 + f] = bot * fin[4 + f]
        sums[6 + f] = jnp.where((lane >= f * 8) & (lane < f * 8 + 8), left, 0.0)
        sums[8 + f] = jnp.where((lane >= 16 + f * 8) & (lane < 24 + f * 8), right, 0.0)
    here = i * NGY + j
    slot = iota((2, 128), 0) * 128 + iota((2, 128), 1)
    row = jnp.zeros((2, 128), F32)
    for n, at in enumerate((here, here - NGY, here + NGY, here - 1, here + 1)):
        for f in range(2):
            total = jnp.sum(sums[2 * n + f], keepdims=True) * (1.0 / 8192.0)
            row = jnp.where(slot == 2 * at + f, total, row)
    send[...] = jnp.broadcast_to(row[None], (NGX * NGY, 2, 128))


def lift_kernel(got, inv, basis, nat, out, coarse):
    q = jnp.sum(got[...], axis=0)
    lane = iota((1, 2), 1)
    pair = jnp.zeros((1, 2), F32)
    for f in range(2):
        c = jnp.sum(q[0:1, :] * inv[0, 0, f : f + 1, 0:128] + q[1:2, :] * inv[0, 0, f : f + 1, 128:256], keepdims=True)
        out[f] = nat[f] + basis[f] * c.reshape(1, 1, 1)
        pair = jnp.where(lane == f, c, pair)
    coarse[0] = pair


def sds(*shape):
    return jax.ShapeDtypeStruct(shape, F32)


def call(kernel, out, scratch=(), **kw):
    vm = pl.BlockSpec(memory_space=pltpu.VMEM)
    return pl.pallas_call(
        kernel,
        out_shape=out,
        scratch_shapes=list(scratch),
        compiler_params=pltpu.CompilerParams(vmem_limit_bytes=48 * 1024 * 1024),
        **kw,
    )


def shift(x, axis, by):
    n = lax.axis_size(axis)
    return lax.ppermute(x, axis, [(k, (k + by) % n) for k in range(n)])


def shards(mixing, forcing, labels, colours, coarse_basis, coarse_inverse):
    vm = pl.BlockSpec(memory_space=pltpu.VMEM)
    coef = lambda t: pltpu.VMEM((8, t, 8, 128), F32)
    block = call(
        pack_kernel, sds(49, 8, 128), in_specs=[vm] * 4 + [pl.BlockSpec(memory_space=pltpu.SMEM)], name="pack"
    )(mixing, forcing, labels, coarse_basis, colours)
    left = shift(block, "gy", 1)
    right = shift(block, "gy", -1)
    up, down = call(rows_kernel, (sds(27, 8, 384), sds(27, 8, 384)), name="rows")(block, left, right, coarse_basis)
    above = shift(down, "gx", 1)
    below = shift(up, "gx", -1)
    msg = lambda r: sds(128 + 2 * KEEP[r], 128)
    stat, u, meta, fin, up, down = call(
        start_kernel,
        (sds(5, ROWS, 128), sds(2, ROWS, 128), sds(24, 128), sds(6, 8, 128), msg(0), msg(0)),
        [pltpu.VMEM((2, 128, 128), F32), pltpu.VMEM((2, ROWS, 128), F32), coef(17), coef(16), coef(16)],
        name="round0",
    )(block, left, right, above, below)
    for rnd in range(1, 5):
        above = shift(down, "gx", 1)
        below = shift(up, "gx", -1)
        u, up, down = call(
            lambda *refs, rnd=rnd: middle_kernel(rnd, *refs),
            (sds(2, ROWS, 128), msg(rnd), msg(rnd)),
            [pltpu.VMEM((2, ROWS, 128), F32), coef(17), coef(16), coef(16)],
            name=f"round{rnd}",
        )(stat, u, meta, above, below)
    above = shift(down, "gx", 1)
    below = shift(up, "gx", -1)
    nat, send = call(
        last_kernel,
        (sds(2, 8, 8, 128), sds(NGX * NGY, 2, 128)),
        [pltpu.VMEM((2, ROWS, 128), F32), pltpu.VMEM((2, ROWS, 128), F32), coef(17)],
        name="round5",
    )(stat, u, meta, above, below, fin, mixing, forcing, labels, coarse_basis)
    got = lax.all_to_all(send, ("gx", "gy"), 0, 0, tiled=True)
    return call(lift_kernel, (sds(2, 8, 8, 128), sds(1, 1, 2)), name="lift")(got, coarse_inverse, coarse_basis, nat)


def solution(mesh):
    return jax.shard_map(
        shards,
        mesh=mesh,
        in_specs=(
            P(None, None, "gx", "gy"),
            P(None, None, "gx", "gy"),
            P(None, "gx", "gy"),
            P("gx", "gy"),
            P(None, None, "gx", "gy"),
            P("gx", "gy", None, None),
        ),
        out_specs=(P(None, None, "gx", "gy"), P("gx", "gy", None)),
        check_vma=False,
    )
```

```python
import jax
import jax.numpy as jnp
from jax import lax
from jax.experimental import pallas as pl
from jax.experimental.pallas import tpu as pltpu
from jax.sharding import PartitionSpec as P

SWEEPS = 20
OMEGA = 0.8
UNROLL = 19
PAD = 8
WIN = (16, 13, 10, 7, 4)
KEEP = (104, 80, 56, 32, 8)
ROWS = 400
F32 = jnp.float32
NGX = 16
NGY = 8


def iota(shape, dim):
    return lax.broadcasted_iota(jnp.int32, shape, dim)


def roll(x, by, axis):
    by = by % x.shape[axis]
    return x if by == 0 else pltpu.roll(x, by, axis)


def lane_ids():
    lane = iota((8, 128), 1)
    return lane & 15, lane >> 4


def edge_columns(tiles):
    lane = iota((8, 128), 1)
    out = jnp.zeros((8, 128), F32)
    for n, tile in enumerate(tiles):
        out = jnp.where(lane == n, roll(tile, n, 1), out)
        out = jnp.where(lane == 16 + n, roll(tile, 17 + n, 1), out)
    return out


def pack_kernel(mix, forc, lab, basis, colour, out, lab_v, basis_v, colour_v, sems):
    copies = [
        pltpu.make_async_copy(basis, basis_v, sems.at[0]),
        pltpu.make_async_copy(lab, lab_v, sems.at[1]),
        pltpu.make_async_copy(colour, colour_v, sems.at[2]),
    ]
    for f in range(3):
        copies.append(pltpu.make_async_copy(mix.at[f], out.at[pl.ds(f * 8, 8)], sems.at[3 + f]))
    for f in range(2):
        copies.append(pltpu.make_async_copy(forc.at[f], out.at[pl.ds(24 + f * 8, 8)], sems.at[6 + f]))
    for c in copies:
        c.start()
    for c in copies:
        c.wait()
    out[40:48] = lab_v[...].astype(F32)
    cols = edge_columns([basis_v[f, z] for f in range(2) for z in range(8)])
    lane = iota((8, 128), 1)
    out[48] = jnp.where(lane == 32, jnp.broadcast_to(colour_v[...].astype(F32), (8, 128)), cols)


def rows_kernel(own, left, right, basis, up, down):
    for part, ref in enumerate((left, own, right)):
        lanes = slice(part * 128, part * 128 + 128)
        for a in range(6):
            for p in range(4):
                lo, hi = ref[a * 8 + 2 * p], ref[a * 8 + 2 * p + 1]
                sub = iota((8, 128), 0)
                up[a * 4 + p, :, lanes] = jnp.where(sub < 4, lo, roll(hi, 4, 0))
                down[a * 4 + p, :, lanes] = jnp.where(sub < 4, roll(lo, 4, 0), hi)
        for z in range(8):
            up[24, z : z + 1, lanes] = ref[40 + z, 4:5, :]
            down[24, z : z + 1, lanes] = ref[40 + z, 3:4, :]
            for f in range(2):
                if part == 1:
                    up[25 + f, z : z + 1, lanes] = basis[f, z, 0:1, :]
                    down[25 + f, z : z + 1, lanes] = basis[f, z, 7:8, :]
        if part != 1:
            up[25:27, :, lanes] = jnp.zeros((2, 8, 128), F32)
            down[25:27, :, lanes] = jnp.zeros((2, 8, 128), F32)


def window_rows(kind, tiles):
    if kind == 0:
        return PAD + 128 - 4
    if kind == 1:
        return PAD + 128 + 4 - 8 * tiles
    return PAD + 128 + 124


def prepare(kind, tiles, stat, u, uo, coef, i, j):
    row0 = window_rows(kind, tiles)
    xp, z = lane_ids()
    sub = iota((8, 128), 0)
    rim_x = ((xp == 0) | (xp == 15)).astype(F32)
    gx = i * 8 + xp - 4
    in_x = ((gx >= 0) & (gx < NGX * 8)).astype(F32)
    for t in range(tiles):
        at = pl.ds(row0 + t, 8, stride=tiles)
        s11, s22, s12 = stat[0, at, :], stat[1, at, :], stat[2, at, :]
        y = row0 - PAD - 128 + sub * tiles + t + j * 128
        inside = in_x * ((y >= 0) & (y < NGY * 128)).astype(F32)
        diag = 6.0 + rim_x
        if t == 0 and kind != 1:
            diag = diag + (sub == 0).astype(F32)
        if t == tiles - 1 and kind != 2:
            diag = diag + (sub == 7).astype(F32)
        vals = []
        for f in range(2):
            c = u[f, at, :]
            near = u[f, pl.ds(row0 + t - 1, 8, stride=tiles), :] + u[f, pl.ds(row0 + t + 1, 8, stride=tiles), :]
            out = uo[f, at, :]
            near = near + jnp.where(xp == 0, out, roll(c, 1, 1)) + jnp.where(xp == 15, out, roll(c, -1, 1))
            near = near + jnp.where(z == 0, 0.0, roll(c, 16, 1)) + jnp.where(z == 7, 0.0, roll(c, -16, 1))
            vals.append((c, near))
        for f, s in ((0, s11), (1, s22)):
            c, near = vals[f]
            r = stat[3 + f, at, :] - ((s + 6.0) * c + s12 * vals[1 - f][0] - near)
            w = OMEGA * inside / (s + diag)
            coef[f, t] = w
            coef[2 + f, t] = w * s12
            coef[4 + f, t] = w * r


def adjacency():
    a, b = iota((128, 128), 0), iota((128, 128), 1)
    ax, az, bx, bz = a & 15, a >> 4, b & 15, b >> 4
    near_x = (az == bz) & ((ax - bx == 1) | (bx - ax == 1))
    near_z = (ax == bx) & ((az - bz == 1) | (bz - az == 1))
    one = (near_x | near_z).astype(F32).astype(jnp.bfloat16)
    return jnp.concatenate([one, one], 0)


def sweep(e, tiles, coef, adj):
    sub = iota((8, 128), 0)
    flat = jnp.concatenate(e[0] + e[1], 0)
    hi = flat.astype(jnp.bfloat16)
    lo = (flat - hi.astype(F32)).astype(jnp.bfloat16)
    side = jnp.dot(jnp.concatenate([hi, lo], 1), adj, preferred_element_type=F32)
    new = [[], []]
    for f in range(2):
        for t in range(tiles):
            c = e[f][t]
            before = e[f][t - 1] if t else jnp.where(sub == 0, 0.0, roll(e[f][tiles - 1], 1, 0))
            after = e[f][t + 1] if t + 1 < tiles else jnp.where(sub == 7, 0.0, roll(e[f][0], -1, 0))
            at = (f * tiles + t) * 8
            near = before + after + side[at : at + 8]
            new[f].append((1.0 - OMEGA) * c + coef[4 + f, t] + (coef[f, t] * near - coef[2 + f, t] * e[1 - f][t]))
    return new


def sweeps(kind, tiles, u, coef):
    row0 = window_rows(kind, tiles)
    xp, z = lane_ids()
    sub = iota((8, 128), 0)
    adj = adjacency()

    def body(_, flat):
        e = [list(flat[:tiles]), list(flat[tiles:])]
        for _ in range(UNROLL):
            e = sweep(e, tiles, coef, adj)
        return tuple(e[0] + e[1])

    flat = tuple(coef[4 + f, t] for f in range(2) for t in range(tiles))
    for _ in range((SWEEPS - 1) % UNROLL):
        e = sweep([list(flat[:tiles]), list(flat[tiles:])], tiles, coef, adj)
        flat = tuple(e[0] + e[1])
    if SWEEPS - 1 == UNROLL:
        flat = body(0, flat)
    else:
        flat = lax.fori_loop(0, (SWEEPS - 1) // UNROLL, body, flat)
    own_x = (xp >= 4) & (xp < 12)
    for t in range(tiles):
        at = pl.ds(row0 + t, 8, stride=tiles)
        y = row0 - PAD - 128 + sub * tiles + t
        if kind == 0:
            here = own_x & (y >= 0) & (y < 128)
        elif kind == 1:
            here = own_x & (y < 0)
        else:
            here = own_x & (y >= 128)
        for f in range(2):
            u[f, at, :] = u[f, at, :] + jnp.where(here, flat[f * tiles + t], 0.0)


def solve_round(rnd, stat, u, uo, meta, coefs, i, j):
    own = jnp.max(meta[0:8, :])
    left = jnp.max(meta[8:16, :])
    right = jnp.max(meta[16:24, :])
    jobs = [(0, 17, own, coefs[0])]
    if rnd < 5:
        jobs += [(1, WIN[rnd], left, coefs[1]), (2, WIN[rnd], right, coefs[2])]
    for kind, tiles, colour, coef in jobs:
        pl.when(colour == float(rnd))(lambda kind=kind, tiles=tiles, coef=coef: prepare(kind, tiles, stat, u, uo, coef, i, j))
    for kind, tiles, colour, coef in jobs:
        pl.when(colour == float(rnd))(lambda kind=kind, tiles=tiles, coef=coef: sweeps(kind, tiles, u, coef))


def emit(rnd, u, up, down):
    keep = KEEP[rnd]
    xp, _ = lane_ids()
    for q in range((128 + 2 * keep) // 8):
        src = pl.ds(PAD + 128 - keep + 8 * q, 8)
        a, b = u[0, src, :], u[1, src, :]
        up[pl.ds(8 * q, 8), :] = jnp.where(xp < 5, roll(a, -4, 1), roll(b, 1, 1))
        down[pl.ds(8 * q, 8), :] = jnp.where(xp < 5, roll(a, -7, 1), roll(b, -2, 1))


def absorb(rnd, u, uo, above, below, i):
    keep = KEEP[rnd]
    xp, _ = lane_ids()
    has_above = (i > 0).astype(F32)
    has_below = (i < NGX - 1).astype(F32)
    for q in range((128 + 2 * keep) // 8):
        at = pl.ds(PAD + 128 - keep + 8 * q, 8)
        a = above[pl.ds(8 * q, 8), :] * has_above
        b = below[pl.ds(8 * q, 8), :] * has_below
        u[0, at, :] = jnp.where(xp < 4, roll(a, -1, 1), jnp.where(xp >= 12, roll(b, 12, 1), u[0, at, :]))
        u[1, at, :] = jnp.where(xp < 4, roll(a, -6, 1), jnp.where(xp >= 12, roll(b, 7, 1), u[1, at, :]))
        uo[0, at, :] = jnp.where(xp == 0, a, roll(b, 11, 1))
        uo[1, at, :] = jnp.where(xp == 0, roll(a, -5, 1), roll(b, 6, 1))


def start_kernel(own, left, right, above, below, stat, u, meta, fin, up, down, buf, uo, c0, c1, c2):
    i = lax.axis_index("gx")
    j = lax.axis_index("gy")
    xp, _ = lane_ids()
    lane = iota((8, 128), 1)
    full_lane = iota((128, 128), 1)
    full_xp = full_lane & 15
    gx = i * 8 + full_xp - 4
    in_x = (gx >= 0) & (gx < NGX * 8)
    for n, ref in enumerate((own, left, right)):
        valid = ((j > 0) if n == 1 else (j < NGY - 1)) if n else (j >= 0)
        colour = jnp.where(lane == 32, jnp.where(valid, 1.0, 0.0) * (ref[48] + 1.0), 0.0) - 1.0
        meta[n * 8 : n * 8 + 8, :] = colour
    fin[0] = left[48] * (j > 0).astype(F32)
    fin[1] = right[48] * (j < NGY - 1).astype(F32)
    for f in range(2):
        fin[2 + f] = above[25 + f, :, 128:256] * (i > 0).astype(F32)
        fin[4 + f] = below[25 + f, :, 128:256] * (i < NGX - 1).astype(F32)
    for f in range(2):
        u[f, 0:PAD, :] = jnp.zeros((PAD, 128), F32)
        u[f, ROWS - PAD : ROWS, :] = jnp.zeros((PAD, 128), F32)
    for part, ref in enumerate((left, own, right)):
        lanes = slice(part * 128, part * 128 + 128)
        rows = slice(PAD + part * 128, PAD + part * 128 + 128)
        gy = (j - 1 + part) * 128
        in_y = (gy >= 0) & (gy < NGY * 128)

        def gather(a):
            slot = a % 2
            for p in range(4):
                for h in range(2):
                    z = 2 * p + h
                    buf[slot, z * 16 : z * 16 + 4, :] = above[a * 4 + p, 4 * h : 4 * h + 4, lanes]
                    buf[slot, z * 16 + 4 : z * 16 + 12, :] = ref[a * 8 + z]
                    buf[slot, z * 16 + 12 : z * 16 + 16, :] = below[a * 4 + p, 4 * h : 4 * h + 4, lanes]
            return buf[slot].T

        stat[0, rows, :] = gather(0)
        stat[1, rows, :] = gather(1)
        stat[2, rows, :] = 0.25 * (gather(2) - 0.125)
        force = [gather(3), gather(4)]
        label = gather(5)
        buf[0] = jnp.zeros((128, 128), F32)
        for z in range(8):
            buf[0, z * 16 : z * 16 + 1, :] = above[24, z : z + 1, lanes]
            buf[0, z * 16 + 15 : z * 16 + 16, :] = below[24, z : z + 1, lanes]
        outer = buf[0].T
        y_ok = in_y.astype(F32)
        out_ok = jnp.where(full_xp == 0, (i > 0).astype(F32), (i < NGX - 1).astype(F32)) * y_ok
        for f in range(2):
            hot = (label == f + 1.0).astype(F32) * (in_x.astype(F32) * y_ok)
            u[f, rows, :] = hot
            stat[3 + f, rows, :] = hot + force[f]
            uo[f, rows, :] = (outer == f + 1.0).astype(F32) * out_ok
    solve_round(0, stat, u, uo, meta, (c0, c1, c2), i, j)
    emit(0, u, up, down)


def middle_kernel(rnd, stat, u_in, meta, above, below, u, up, down, uo, c0, c1, c2):
    i = lax.axis_index("gx")
    j = lax.axis_index("gy")
    u[...] = u_in[...]
    absorb(rnd - 1, u, uo, above, below, i)
    solve_round(rnd, stat, u, uo, meta, (c0, c1, c2), i, j)
    emit(rnd, u, up, down)


def last_kernel(stat, u_in, meta, above, below, fin, mix, forc, lab, basis, nat, send, u, uo, c0):
    i = lax.axis_index("gx")
    j = lax.axis_index("gy")
    u[...] = u_in[...]
    absorb(4, u, uo, above, below, i)
    solve_round(5, stat, u, uo, meta, (c0,), i, j)
    sub = iota((8, 128), 0)
    lane = iota((8, 128), 1)
    tiles = []
    for f in range(2):
        flat = u[f, PAD + 128 : PAD + 256, :].T
        for z in range(8):
            tile = flat[z * 16 + 4 : z * 16 + 12, :]
            nat[f, z] = tile
            tiles.append(tile)
    cols = edge_columns(tiles)
    sums = [jnp.zeros((8, 128), F32) for _ in range(10)]
    left = cols * roll(fin[0], -16, 1)
    right = cols * roll(fin[1], 16, 1)
    for f in range(2):
        acc = jnp.zeros((8, 128), F32)
        for z in range(8):
            c, other = tiles[f * 8 + z], tiles[(1 - f) * 8 + z]
            near = jnp.where(sub == 0, 0.0, roll(c, 1, 0)) + jnp.where(sub == 7, 0.0, roll(c, -1, 0))
            near = near + jnp.where(lane == 0, 0.0, roll(c, 1, 1)) + jnp.where(lane == 127, 0.0, roll(c, -1, 1))
            if z > 0:
                near = near + tiles[f * 8 + z - 1]
            if z < 7:
                near = near + tiles[f * 8 + z + 1]
            s12 = 0.25 * (mix[2, z] - 0.125)
            rhs = (lab[z] == f + 1).astype(F32) + forc[f, z]
            acc = acc + basis[f, z] * (rhs - ((mix[f, z] + 6.0) * c + s12 * other - near))
        sums[f] = acc
        top = jnp.zeros((8, 128), F32)
        bot = jnp.zeros((8, 128), F32)
        for z in range(8):
            top = jnp.where(sub == z, jnp.broadcast_to(tiles[f * 8 + z][0:1, :], (8, 128)), top)
            bot = jnp.where(sub == z, jnp.broadcast_to(tiles[f * 8 + z][7:8, :], (8, 128)), bot)
        sums[2 + f] = top * fin[2 + f]
        sums[4 + f] = bot * fin[4 + f]
        sums[6 + f] = jnp.where((lane >= f * 8) & (lane < f * 8 + 8), left, 0.0)
        sums[8 + f] = jnp.where((lane >= 16 + f * 8) & (lane < 24 + f * 8), right, 0.0)
    here = i * NGY + j
    slot = iota((2, 128), 0) * 128 + iota((2, 128), 1)
    row = jnp.zeros((2, 128), F32)
    for n, at in enumerate((here, here - NGY, here + NGY, here - 1, here + 1)):
        for f in range(2):
            total = jnp.sum(sums[2 * n + f], keepdims=True) * (1.0 / 8192.0)
            row = jnp.where(slot == 2 * at + f, total, row)
    send[...] = jnp.broadcast_to(row[None], (NGX * NGY, 2, 128))


def lift_kernel(got, inv, basis, nat, out, coarse):
    q = jnp.sum(got[...], axis=0)
    lane = iota((1, 2), 1)
    pair = jnp.zeros((1, 2), F32)
    for f in range(2):
        c = jnp.sum(q[0:1, :] * inv[0, 0, f : f + 1, 0:128] + q[1:2, :] * inv[0, 0, f : f + 1, 128:256], keepdims=True)
        out[f] = nat[f] + basis[f] * c.reshape(1, 1, 1)
        pair = jnp.where(lane == f, c, pair)
    coarse[0] = pair


def sds(*shape):
    return jax.ShapeDtypeStruct(shape, F32)


def call(kernel, out, scratch=(), **kw):
    return pl.pallas_call(
        kernel,
        out_shape=out,
        scratch_shapes=list(scratch),
        compiler_params=pltpu.CompilerParams(vmem_limit_bytes=48 * 1024 * 1024),
        **kw,
    )


def shift(x, axis, by):
    n = lax.axis_size(axis)
    return lax.ppermute(x, axis, [(k, (k + by) % n) for k in range(n)])


def shards(mixing, forcing, labels, colours, coarse_basis, coarse_inverse):
    coef = lambda t: pltpu.VMEM((6, t, 8, 128), F32)
    block = call(
        pack_kernel,
        sds(49, 8, 128),
        [
            pltpu.VMEM((8, 8, 128), jnp.int32),
            pltpu.VMEM((2, 8, 8, 128), F32),
            pltpu.VMEM((1, 1), jnp.int32),
            pltpu.SemaphoreType.DMA((8,)),
        ],
        in_specs=[pl.BlockSpec(memory_space=pl.ANY)] * 5,
        name="pack",
    )(mixing, forcing, labels, coarse_basis, colours)
    left = shift(block, "gy", 1)
    right = shift(block, "gy", -1)
    up, down = call(rows_kernel, (sds(27, 8, 384), sds(27, 8, 384)), name="rows")(block, left, right, coarse_basis)
    above = shift(down, "gx", 1)
    below = shift(up, "gx", -1)
    msg = lambda r: sds(128 + 2 * KEEP[r], 128)
    stat, u, meta, fin, up, down = call(
        start_kernel,
        (sds(5, ROWS, 128), sds(2, ROWS, 128), sds(24, 128), sds(6, 8, 128), msg(0), msg(0)),
        [pltpu.VMEM((2, 128, 128), F32), pltpu.VMEM((2, ROWS, 128), F32), coef(17), coef(16), coef(16)],
        name="round0",
    )(block, left, right, above, below)
    for rnd in range(1, 5):
        above = shift(down, "gx", 1)
        below = shift(up, "gx", -1)
        u, up, down = call(
            lambda *refs, rnd=rnd: middle_kernel(rnd, *refs),
            (sds(2, ROWS, 128), msg(rnd), msg(rnd)),
            [pltpu.VMEM((2, ROWS, 128), F32), coef(17), coef(16), coef(16)],
            name=f"round{rnd}",
        )(stat, u, meta, above, below)
    above = shift(down, "gx", 1)
    below = shift(up, "gx", -1)
    nat, send = call(
        last_kernel,
        (sds(2, 8, 8, 128), sds(NGX * NGY, 2, 128)),
        [pltpu.VMEM((2, ROWS, 128), F32), pltpu.VMEM((2, ROWS, 128), F32), coef(17)],
        name="round5",
    )(stat, u, meta, above, below, fin, mixing, forcing, labels, coarse_basis)
    got = lax.all_to_all(send, ("gx", "gy"), 0, 0, tiled=True)
    return call(lift_kernel, (sds(2, 8, 8, 128), sds(1, 1, 2)), name="lift")(got, coarse_inverse, coarse_basis, nat)


def solution(mesh):
    return jax.shard_map(
        shards,
        mesh=mesh,
        in_specs=(
            P(None, None, "gx", "gy"),
            P(None, None, "gx", "gy"),
            P(None, "gx", "gy"),
            P("gx", "gy"),
            P(None, None, "gx", "gy"),
            P("gx", "gy", None, None),
        ),
        out_specs=(P(None, None, "gx", "gy"), P("gx", "gy", None)),
        check_vma=False,
    )
```

```python
import jax
import jax.numpy as jnp
from jax import lax
from jax.experimental import pallas as pl
from jax.experimental.pallas import tpu as pltpu
from jax.sharding import PartitionSpec as P

SWEEPS = 20
OMEGA = 0.8
UNROLL = 19
PAD = 8
WIN = (16, 13, 10, 7, 4)
KEEP = (104, 80, 56, 32, 8)
ROWS = 400
F32 = jnp.float32
NGX = 16
NGY = 8


def iota(shape, dim):
    return lax.broadcasted_iota(jnp.int32, shape, dim)


def roll(x, by, axis):
    by = by % x.shape[axis]
    return x if by == 0 else pltpu.roll(x, by, axis)


def lane_ids():
    lane = iota((8, 128), 1)
    return lane & 15, lane >> 4


def edge_columns(tiles):
    lane = iota((8, 128), 1)
    out = jnp.zeros((8, 128), F32)
    for n, tile in enumerate(tiles):
        out = jnp.where(lane == n, roll(tile, n, 1), out)
        out = jnp.where(lane == 16 + n, roll(tile, 17 + n, 1), out)
    return out


def pack_kernel(mix, forc, lab, basis, colour, out, lab_v, basis_v, sems):
    copies = [
        pltpu.make_async_copy(basis, basis_v, sems.at[0]),
        pltpu.make_async_copy(lab, lab_v, sems.at[1]),
    ]
    for f in range(3):
        copies.append(pltpu.make_async_copy(mix.at[f], out.at[pl.ds(f * 8, 8)], sems.at[3 + f]))
    for f in range(2):
        copies.append(pltpu.make_async_copy(forc.at[f], out.at[pl.ds(24 + f * 8, 8)], sems.at[6 + f]))
    for c in copies:
        c.start()
    for c in copies:
        c.wait()
    out[40:48] = lab_v[...].astype(F32)
    cols = edge_columns([basis_v[f, z] for f in range(2) for z in range(8)])
    lane = iota((8, 128), 1)
    out[48] = jnp.where(lane == 32, colour[...].astype(F32), cols)


def rows_kernel(own, left, right, basis, first, second):
    even = lax.axis_index("gx") % 2 == 0
    pl.when(even)(lambda: write_rows(own, left, right, basis, second, first))
    pl.when(jnp.logical_not(even))(lambda: write_rows(own, left, right, basis, first, second))


def write_rows(own, left, right, basis, up, down):
    for part, ref in enumerate((left, own, right)):
        lanes = slice(part * 128, part * 128 + 128)
        for a in range(6):
            for p in range(4):
                lo, hi = ref[a * 8 + 2 * p], ref[a * 8 + 2 * p + 1]
                sub = iota((8, 128), 0)
                up[a * 4 + p, :, lanes] = jnp.where(sub < 4, lo, roll(hi, 4, 0))
                down[a * 4 + p, :, lanes] = jnp.where(sub < 4, roll(lo, 4, 0), hi)
        for z in range(8):
            up[24, z : z + 1, lanes] = ref[40 + z, 4:5, :]
            down[24, z : z + 1, lanes] = ref[40 + z, 3:4, :]
            for f in range(2):
                if part == 1:
                    up[25 + f, z : z + 1, lanes] = basis[f, z, 0:1, :]
                    down[25 + f, z : z + 1, lanes] = basis[f, z, 7:8, :]
        if part != 1:
            up[25:27, :, lanes] = jnp.zeros((2, 8, 128), F32)
            down[25:27, :, lanes] = jnp.zeros((2, 8, 128), F32)


def window_rows(kind, tiles):
    if kind == 0:
        return PAD + 128 - 4
    if kind == 1:
        return PAD + 128 + 4 - 8 * tiles
    return PAD + 128 + 124


def prepare(kind, tiles, stat, u, uo, coef, i, j):
    row0 = window_rows(kind, tiles)
    xp, z = lane_ids()
    sub = iota((8, 128), 0)
    rim_x = ((xp == 0) | (xp == 15)).astype(F32)
    gx = i * 8 + xp - 4
    in_x = ((gx >= 0) & (gx < NGX * 8)).astype(F32)
    for t in range(tiles):
        at = pl.ds(row0 + t, 8, stride=tiles)
        s11, s22, s12 = stat[0, at, :], stat[1, at, :], stat[2, at, :]
        y = row0 - PAD - 128 + sub * tiles + t + j * 128
        inside = in_x * ((y >= 0) & (y < NGY * 128)).astype(F32)
        diag = 6.0 + rim_x
        if t == 0 and kind != 1:
            diag = diag + (sub == 0).astype(F32)
        if t == tiles - 1 and kind != 2:
            diag = diag + (sub == 7).astype(F32)
        vals = []
        for f in range(2):
            c = u[f, at, :]
            near = u[f, pl.ds(row0 + t - 1, 8, stride=tiles), :] + u[f, pl.ds(row0 + t + 1, 8, stride=tiles), :]
            out = uo[f, at, :]
            near = near + jnp.where(xp == 0, out, roll(c, 1, 1)) + jnp.where(xp == 15, out, roll(c, -1, 1))
            near = near + jnp.where(z == 0, 0.0, roll(c, 16, 1)) + jnp.where(z == 7, 0.0, roll(c, -16, 1))
            vals.append((c, near))
        for f, s in ((0, s11), (1, s22)):
            c, near = vals[f]
            r = stat[3 + f, at, :] - ((s + 6.0) * c + s12 * vals[1 - f][0] - near)
            w = OMEGA * inside / (s + diag)
            coef[f, t] = w
            coef[2 + f, t] = w * s12
            coef[4 + f, t] = w * r


def adjacency():
    a, b = iota((128, 128), 0), iota((128, 128), 1)
    ax, az, bx, bz = a & 15, a >> 4, b & 15, b >> 4
    near_x = (az == bz) & ((ax - bx == 1) | (bx - ax == 1))
    near_z = (ax == bx) & ((az - bz == 1) | (bz - az == 1))
    one = (near_x | near_z).astype(F32).astype(jnp.bfloat16)
    return jnp.concatenate([one, one], 0)


def sweep(e, tiles, coef, adj):
    sub = iota((8, 128), 0)
    flat = jnp.concatenate(e[0] + e[1], 0)
    hi = flat.astype(jnp.bfloat16)
    lo = (flat - hi.astype(F32)).astype(jnp.bfloat16)
    side = jnp.dot(jnp.concatenate([hi, lo], 1), adj, preferred_element_type=F32)
    new = [[], []]
    for f in range(2):
        for t in range(tiles):
            c = e[f][t]
            before = e[f][t - 1] if t else jnp.where(sub == 0, 0.0, roll(e[f][tiles - 1], 1, 0))
            after = e[f][t + 1] if t + 1 < tiles else jnp.where(sub == 7, 0.0, roll(e[f][0], -1, 0))
            at = (f * tiles + t) * 8
            near = before + after + side[at : at + 8]
            new[f].append((1.0 - OMEGA) * c + coef[4 + f, t] + (coef[f, t] * near - coef[2 + f, t] * e[1 - f][t]))
    return new


def sweeps(kind, tiles, u, coef):
    row0 = window_rows(kind, tiles)
    xp, z = lane_ids()
    sub = iota((8, 128), 0)
    adj = adjacency()

    def body(_, flat):
        e = [list(flat[:tiles]), list(flat[tiles:])]
        for _ in range(UNROLL):
            e = sweep(e, tiles, coef, adj)
        return tuple(e[0] + e[1])

    flat = tuple(coef[4 + f, t] for f in range(2) for t in range(tiles))
    for _ in range((SWEEPS - 1) % UNROLL):
        e = sweep([list(flat[:tiles]), list(flat[tiles:])], tiles, coef, adj)
        flat = tuple(e[0] + e[1])
    if SWEEPS - 1 == UNROLL:
        flat = body(0, flat)
    else:
        flat = lax.fori_loop(0, (SWEEPS - 1) // UNROLL, body, flat)
    own_x = (xp >= 4) & (xp < 12)
    for t in range(tiles):
        at = pl.ds(row0 + t, 8, stride=tiles)
        y = row0 - PAD - 128 + sub * tiles + t
        if kind == 0:
            here = own_x & (y >= 0) & (y < 128)
        elif kind == 1:
            here = own_x & (y < 0)
        else:
            here = own_x & (y >= 128)
        for f in range(2):
            u[f, at, :] = u[f, at, :] + jnp.where(here, flat[f * tiles + t], 0.0)


def solve_round(rnd, stat, u, uo, meta, coefs, i, j):
    own = jnp.max(meta[0:8, :])
    left = jnp.max(meta[8:16, :])
    right = jnp.max(meta[16:24, :])
    jobs = [(0, 17, own, coefs[0])]
    if rnd < 5:
        jobs += [(1, WIN[rnd], left, coefs[1]), (2, WIN[rnd], right, coefs[2])]
    for kind, tiles, colour, coef in jobs:
        pl.when(colour == float(rnd))(lambda kind=kind, tiles=tiles, coef=coef: prepare(kind, tiles, stat, u, uo, coef, i, j))
    for kind, tiles, colour, coef in jobs:
        pl.when(colour == float(rnd))(lambda kind=kind, tiles=tiles, coef=coef: sweeps(kind, tiles, u, coef))


def message_items(rnd):
    tiles = (128 + 2 * KEEP[rnd]) // 8
    items = [(f, PAD + 128 - KEEP[rnd] + 8 * q) for f in range(2) for q in range(tiles)]
    third = len(items) // 3
    return [[items[g * third + m] for g in range(3)] for m in range(third)]


def emit(rnd, u, first, second, even):
    xp, _ = lane_ids()

    def write(up, down):
        for m, trio in enumerate(message_items(rnd)):
            tiles = [u[f, pl.ds(row, 8), :] for f, row in trio]
            at = pl.ds(8 * m, 8)
            for ref, lane0 in ((up, 4), (down, 7)):
                a, b, c = (roll(tile, 5 * g - lane0, 1) for g, tile in enumerate(tiles))
                ref[at, :] = jnp.where(xp < 5, a, jnp.where(xp < 10, b, c))

    pl.when(even)(lambda: write(second, first))
    pl.when(jnp.logical_not(even))(lambda: write(first, second))


def absorb(rnd, u, uo, first, second, i):
    xp, _ = lane_ids()
    has_above = (i > 0).astype(F32)
    has_below = (i < NGX - 1).astype(F32)

    def read(above, below):
        for m, trio in enumerate(message_items(rnd)):
            a = above[pl.ds(8 * m, 8), :] * has_above
            b = below[pl.ds(8 * m, 8), :] * has_below
            for g, (f, row) in enumerate(trio):
                at = pl.ds(row, 8)
                inner = jnp.where(xp >= 12, roll(b, 12 - 5 * g, 1), u[f, at, :])
                u[f, at, :] = jnp.where(xp < 4, roll(a, -5 * g - 1, 1), inner)
                uo[f, at, :] = jnp.where(xp == 0, roll(a, -5 * g, 1), roll(b, 11 - 5 * g, 1))

    even = i % 2 == 0
    pl.when(even)(lambda: read(second, first))
    pl.when(jnp.logical_not(even))(lambda: read(first, second))


def start_kernel(own, left, right, first, second, stat, u, meta, fin, out1, out2, near, buf, uo, c0, c1, c2):
    i = lax.axis_index("gx")
    even = i % 2 == 0

    def place(above, below):
        near[0] = above[...]
        near[1] = below[...]

    pl.when(even)(lambda: place(second, first))
    pl.when(jnp.logical_not(even))(lambda: place(first, second))
    above, below = near.at[0], near.at[1]
    j = lax.axis_index("gy")
    xp, _ = lane_ids()
    lane = iota((8, 128), 1)
    full_lane = iota((128, 128), 1)
    full_xp = full_lane & 15
    gx = i * 8 + full_xp - 4
    in_x = (gx >= 0) & (gx < NGX * 8)
    for n, ref in enumerate((own, left, right)):
        valid = ((j > 0) if n == 1 else (j < NGY - 1)) if n else (j >= 0)
        colour = jnp.where(lane == 32, jnp.where(valid, 1.0, 0.0) * (ref[48] + 1.0), 0.0) - 1.0
        meta[n * 8 : n * 8 + 8, :] = colour
    fin[0] = left[48] * (j > 0).astype(F32)
    fin[1] = right[48] * (j < NGY - 1).astype(F32)
    for f in range(2):
        fin[2 + f] = above[25 + f, :, 128:256] * (i > 0).astype(F32)
        fin[4 + f] = below[25 + f, :, 128:256] * (i < NGX - 1).astype(F32)
    for f in range(2):
        u[f, 0:PAD, :] = jnp.zeros((PAD, 128), F32)
        u[f, ROWS - PAD : ROWS, :] = jnp.zeros((PAD, 128), F32)
    for part, ref in enumerate((left, own, right)):
        lanes = slice(part * 128, part * 128 + 128)
        rows = slice(PAD + part * 128, PAD + part * 128 + 128)
        gy = (j - 1 + part) * 128
        in_y = (gy >= 0) & (gy < NGY * 128)

        def gather(a):
            slot = a % 2
            for p in range(4):
                for h in range(2):
                    z = 2 * p + h
                    buf[slot, z * 16 : z * 16 + 4, :] = above[a * 4 + p, 4 * h : 4 * h + 4, lanes]
                    buf[slot, z * 16 + 4 : z * 16 + 12, :] = ref[a * 8 + z]
                    buf[slot, z * 16 + 12 : z * 16 + 16, :] = below[a * 4 + p, 4 * h : 4 * h + 4, lanes]
            return buf[slot].T

        stat[0, rows, :] = gather(0)
        stat[1, rows, :] = gather(1)
        stat[2, rows, :] = 0.25 * (gather(2) - 0.125)
        force = [gather(3), gather(4)]
        label = gather(5)
        buf[0] = jnp.zeros((128, 128), F32)
        for z in range(8):
            buf[0, z * 16 : z * 16 + 1, :] = above[24, z : z + 1, lanes]
            buf[0, z * 16 + 15 : z * 16 + 16, :] = below[24, z : z + 1, lanes]
        outer = buf[0].T
        y_ok = in_y.astype(F32)
        out_ok = jnp.where(full_xp == 0, (i > 0).astype(F32), (i < NGX - 1).astype(F32)) * y_ok
        for f in range(2):
            hot = (label == f + 1.0).astype(F32) * (in_x.astype(F32) * y_ok)
            u[f, rows, :] = hot
            stat[3 + f, rows, :] = hot + force[f]
            uo[f, rows, :] = (outer == f + 1.0).astype(F32) * out_ok
    solve_round(0, stat, u, uo, meta, (c0, c1, c2), i, j)
    emit(0, u, out1, out2, even)


def middle_kernel(rnd, stat, u_in, meta, first, second, u, out1, out2, uo, c0, c1, c2):
    i = lax.axis_index("gx")
    j = lax.axis_index("gy")
    u[...] = u_in[...]
    absorb(rnd - 1, u, uo, first, second, i)
    solve_round(rnd, stat, u, uo, meta, (c0, c1, c2), i, j)
    emit(rnd, u, out1, out2, i % 2 == 0)


def last_kernel(stat, u_in, meta, first, second, fin, mix, forc, lab, basis, nat, send, u, uo, c0):
    i = lax.axis_index("gx")
    j = lax.axis_index("gy")
    u[...] = u_in[...]
    absorb(4, u, uo, first, second, i)
    solve_round(5, stat, u, uo, meta, (c0,), i, j)
    sub = iota((8, 128), 0)
    lane = iota((8, 128), 1)
    tiles = []
    for f in range(2):
        flat = u[f, PAD + 128 : PAD + 256, :].T
        for z in range(8):
            tile = flat[z * 16 + 4 : z * 16 + 12, :]
            nat[f, z] = tile
            tiles.append(tile)
    cols = edge_columns(tiles)
    sums = [jnp.zeros((8, 128), F32) for _ in range(10)]
    left = cols * roll(fin[0], -16, 1)
    right = cols * roll(fin[1], 16, 1)
    for f in range(2):
        acc = jnp.zeros((8, 128), F32)
        for z in range(8):
            c, other = tiles[f * 8 + z], tiles[(1 - f) * 8 + z]
            near = jnp.where(sub == 0, 0.0, roll(c, 1, 0)) + jnp.where(sub == 7, 0.0, roll(c, -1, 0))
            near = near + jnp.where(lane == 0, 0.0, roll(c, 1, 1)) + jnp.where(lane == 127, 0.0, roll(c, -1, 1))
            if z > 0:
                near = near + tiles[f * 8 + z - 1]
            if z < 7:
                near = near + tiles[f * 8 + z + 1]
            s12 = 0.25 * (mix[2, z] - 0.125)
            rhs = (lab[z] == f + 1).astype(F32) + forc[f, z]
            acc = acc + basis[f, z] * (rhs - ((mix[f, z] + 6.0) * c + s12 * other - near))
        sums[f] = acc
        top = jnp.zeros((8, 128), F32)
        bot = jnp.zeros((8, 128), F32)
        for z in range(8):
            top = jnp.where(sub == z, jnp.broadcast_to(tiles[f * 8 + z][0:1, :], (8, 128)), top)
            bot = jnp.where(sub == z, jnp.broadcast_to(tiles[f * 8 + z][7:8, :], (8, 128)), bot)
        sums[2 + f] = top * fin[2 + f]
        sums[4 + f] = bot * fin[4 + f]
        sums[6 + f] = jnp.where((lane >= f * 8) & (lane < f * 8 + 8), left, 0.0)
        sums[8 + f] = jnp.where((lane >= 16 + f * 8) & (lane < 24 + f * 8), right, 0.0)
    here = i * NGY + j
    slot = iota((2, 128), 0) * 128 + iota((2, 128), 1)
    row = jnp.zeros((2, 128), F32)
    for n, at in enumerate((here, here - NGY, here + NGY, here - 1, here + 1)):
        for f in range(2):
            total = jnp.sum(sums[2 * n + f], keepdims=True) * (1.0 / 8192.0)
            row = jnp.where(slot == 2 * at + f, total, row)
    send[...] = jnp.broadcast_to(row[None], (NGX * NGY, 2, 128))


def lift_kernel(got, inv, basis, nat, out, coarse):
    q = jnp.sum(got[...], axis=0)
    lane = iota((1, 2), 1)
    pair = jnp.zeros((1, 2), F32)
    for f in range(2):
        c = jnp.sum(q[0:1, :] * inv[0, 0, f : f + 1, 0:128] + q[1:2, :] * inv[0, 0, f : f + 1, 128:256], keepdims=True)
        out[f] = nat[f] + basis[f] * c.reshape(1, 1, 1)
        pair = jnp.where(lane == f, c, pair)
    coarse[0] = pair


def sds(*shape):
    return jax.ShapeDtypeStruct(shape, F32)


def call(kernel, out, scratch=(), **kw):
    return pl.pallas_call(
        kernel,
        out_shape=out,
        scratch_shapes=list(scratch),
        compiler_params=pltpu.CompilerParams(vmem_limit_bytes=48 * 1024 * 1024),
        **kw,
    )


def shift(x, axis, by):
    n = lax.axis_size(axis)
    return lax.ppermute(x, axis, [(k, (k + by) % n) for k in range(n)])


def swap(x, odd):
    n = lax.axis_size("gx")
    return lax.ppermute(x, "gx", [(k, (((k + odd) ^ 1) - odd) % n) for k in range(n)])


def shards(mixing, forcing, labels, colours, coarse_basis, coarse_inverse):
    coef = lambda t: pltpu.VMEM((6, t, 8, 128), F32)
    block = call(
        pack_kernel,
        sds(49, 8, 128),
        [
            pltpu.VMEM((8, 8, 128), jnp.int32),
            pltpu.VMEM((2, 8, 8, 128), F32),
            pltpu.SemaphoreType.DMA((8,)),
        ],
        in_specs=[pl.BlockSpec(memory_space=pltpu.HBM)] * 4 + [pl.BlockSpec(memory_space=pltpu.VMEM)],
        name="pack",
    )(
        *(pltpu.with_memory_space_constraint(x, pltpu.HBM) for x in (mixing, forcing, labels, coarse_basis)),
        jnp.broadcast_to(colours, (8, 128)),
    )
    left = shift(block, "gy", 1)
    right = shift(block, "gy", -1)
    one, two = call(rows_kernel, (sds(27, 8, 384), sds(27, 8, 384)), name="rows")(block, left, right, coarse_basis)
    one, two = swap(one, 0), swap(two, 1)
    msg = lambda r: sds(8 * len(message_items(r)), 128)
    stat, u, meta, fin, one, two = call(
        start_kernel,
        (sds(5, ROWS, 128), sds(2, ROWS, 128), sds(24, 128), sds(6, 8, 128), msg(0), msg(0)),
        [pltpu.VMEM((2, 27, 8, 384), F32), pltpu.VMEM((2, 128, 128), F32), pltpu.VMEM((2, ROWS, 128), F32)]
        + [coef(17), coef(16), coef(16)],
        name="round0",
    )(block, left, right, one, two)
    for rnd in range(1, 5):
        one, two = swap(one, 0), swap(two, 1)
        u, one, two = call(
            lambda *refs, rnd=rnd: middle_kernel(rnd, *refs),
            (sds(2, ROWS, 128), msg(rnd), msg(rnd)),
            [pltpu.VMEM((2, ROWS, 128), F32), coef(17), coef(16), coef(16)],
            name=f"round{rnd}",
        )(stat, u, meta, one, two)
    one, two = swap(one, 0), swap(two, 1)
    nat, send = call(
        last_kernel,
        (sds(2, 8, 8, 128), sds(NGX * NGY, 2, 128)),
        [pltpu.VMEM((2, ROWS, 128), F32), pltpu.VMEM((2, ROWS, 128), F32), coef(17)],
        name="round5",
    )(stat, u, meta, one, two, fin, mixing, forcing, labels, coarse_basis)
    got = lax.all_to_all(send, ("gx", "gy"), 0, 0, tiled=True)
    return call(lift_kernel, (sds(2, 8, 8, 128), sds(1, 1, 2)), name="lift")(got, coarse_inverse, coarse_basis, nat)


def solution(mesh):
    return jax.shard_map(
        shards,
        mesh=mesh,
        in_specs=(
            P(None, None, "gx", "gy"),
            P(None, None, "gx", "gy"),
            P(None, "gx", "gy"),
            P("gx", "gy"),
            P(None, None, "gx", "gy"),
            P("gx", "gy", None, None),
        ),
        out_specs=(P(None, None, "gx", "gy"), P("gx", "gy", None)),
        check_vma=False,
    )
```

```python
import jax
import jax.numpy as jnp
from jax import lax
from jax.experimental import pallas as pl
from jax.experimental.pallas import tpu as pltpu
from jax.sharding import PartitionSpec as P

SWEEPS = 20
OMEGA = 0.8
UNROLL = 19
PAD = 8
WIN = (16, 13, 10, 7, 4)
KEEP = (104, 80, 56, 32, 8)
ROWS = 400
F32 = jnp.float32
NGX = 16
NGY = 8


def home(i, j):
    pair, core = i // 2, i % 2
    y, low = (pair, 0) if pair < 4 else (7 - pair, 1)
    return (y * 4 + j // 4 * 2 + core) * NGY + low * 4 + j % 4


def block_here():
    gx, gy = lax.axis_index("gx"), lax.axis_index("gy")
    y, low = gx // 4, gy // 4
    pair = jnp.where(low == 0, y, 7 - y)
    return pair * 2 + gx % 2, gx // 2 % 2 * 4 + gy % 4


def send(x, to):
    blocks = [(i, j) for i in range(NGX) for j in range(NGY)]
    return lax.ppermute(x, ("gx", "gy"), [to(i, j) for i, j in blocks])


def iota(shape, dim):
    return lax.broadcasted_iota(jnp.int32, shape, dim)


def roll(x, by, axis):
    by = by % x.shape[axis]
    return x if by == 0 else pltpu.roll(x, by, axis)


def lane_ids():
    lane = iota((8, 128), 1)
    return lane & 15, lane >> 4


def edge_columns(tiles):
    lane = iota((8, 128), 1)
    out = jnp.zeros((8, 128), F32)
    for n, tile in enumerate(tiles):
        out = jnp.where(lane == n, roll(tile, n, 1), out)
        out = jnp.where(lane == 16 + n, roll(tile, 17 + n, 1), out)
    return out


def pack_kernel(mix, forc, lab, basis, colour, out, full, lab_v, sems):
    copies = [
        pltpu.make_async_copy(lab, lab_v, sems.at[0]),
        pltpu.make_async_copy(basis.at[0], full.at[pl.ds(49, 8)], sems.at[1]),
        pltpu.make_async_copy(basis.at[1], full.at[pl.ds(57, 8)], sems.at[2]),
    ]
    for f in range(3):
        copies.append(pltpu.make_async_copy(mix.at[f], out.at[pl.ds(f * 8, 8)], sems.at[3 + f]))
    for f in range(2):
        copies.append(pltpu.make_async_copy(forc.at[f], out.at[pl.ds(24 + f * 8, 8)], sems.at[6 + f]))
    for c in copies:
        c.start()
    for c in copies:
        c.wait()
    out[40:48] = lab_v[...].astype(F32)
    cols = edge_columns([full[49 + n] for n in range(16)])
    lane = iota((8, 128), 1)
    out[48] = jnp.where(lane == 32, colour[...].astype(F32), cols)
    full[0:49] = out[...]


def rows_kernel(own, left, right, first, second):
    even = block_here()[0] % 2 == 0
    pl.when(even)(lambda: write_rows(own, left, right, second, first))
    pl.when(jnp.logical_not(even))(lambda: write_rows(own, left, right, first, second))


def write_rows(own, left, right, up, down):
    for part, ref in enumerate((left, own, right)):
        lanes = slice(part * 128, part * 128 + 128)
        for a in range(6):
            for p in range(4):
                lo, hi = ref[a * 8 + 2 * p], ref[a * 8 + 2 * p + 1]
                sub = iota((8, 128), 0)
                up[a * 4 + p, :, lanes] = jnp.where(sub < 4, lo, roll(hi, 4, 0))
                down[a * 4 + p, :, lanes] = jnp.where(sub < 4, roll(lo, 4, 0), hi)
        for z in range(8):
            up[24, z : z + 1, lanes] = ref[40 + z, 4:5, :]
            down[24, z : z + 1, lanes] = ref[40 + z, 3:4, :]
            for f in range(2):
                if part == 1:
                    up[25 + f, z : z + 1, lanes] = own[49 + f * 8 + z, 0:1, :]
                    down[25 + f, z : z + 1, lanes] = own[49 + f * 8 + z, 7:8, :]
        if part != 1:
            up[25:27, :, lanes] = jnp.zeros((2, 8, 128), F32)
            down[25:27, :, lanes] = jnp.zeros((2, 8, 128), F32)


def window_rows(kind, tiles):
    if kind == 0:
        return PAD + 128 - 4
    if kind == 1:
        return PAD + 128 + 4 - 8 * tiles
    return PAD + 128 + 124


def prepare(kind, tiles, stat, u, uo, coef, i, j):
    row0 = window_rows(kind, tiles)
    xp, z = lane_ids()
    sub = iota((8, 128), 0)
    rim_x = ((xp == 0) | (xp == 15)).astype(F32)
    gx = i * 8 + xp - 4
    in_x = ((gx >= 0) & (gx < NGX * 8)).astype(F32)
    for t in range(tiles):
        at = pl.ds(row0 + t, 8, stride=tiles)
        s11, s22, s12 = stat[0, at, :], stat[1, at, :], stat[2, at, :]
        y = row0 - PAD - 128 + sub * tiles + t + j * 128
        inside = in_x * ((y >= 0) & (y < NGY * 128)).astype(F32)
        diag = 6.0 + rim_x
        if t == 0 and kind != 1:
            diag = diag + (sub == 0).astype(F32)
        if t == tiles - 1 and kind != 2:
            diag = diag + (sub == 7).astype(F32)
        vals = []
        for f in range(2):
            c = u[f, at, :]
            near = u[f, pl.ds(row0 + t - 1, 8, stride=tiles), :] + u[f, pl.ds(row0 + t + 1, 8, stride=tiles), :]
            out = uo[f, at, :]
            near = near + jnp.where(xp == 0, out, roll(c, 1, 1)) + jnp.where(xp == 15, out, roll(c, -1, 1))
            near = near + jnp.where(z == 0, 0.0, roll(c, 16, 1)) + jnp.where(z == 7, 0.0, roll(c, -16, 1))
            vals.append((c, near))
        for f, s in ((0, s11), (1, s22)):
            c, near = vals[f]
            r = stat[3 + f, at, :] - ((s + 6.0) * c + s12 * vals[1 - f][0] - near)
            w = OMEGA * inside / (s + diag)
            coef[f, t] = w
            coef[2 + f, t] = w * s12
            coef[4 + f, t] = w * r


def adjacency():
    a, b = iota((128, 128), 0), iota((128, 128), 1)
    ax, az, bx, bz = a & 15, a >> 4, b & 15, b >> 4
    near_x = (az == bz) & ((ax - bx == 1) | (bx - ax == 1))
    near_z = (ax == bx) & ((az - bz == 1) | (bz - az == 1))
    one = (near_x | near_z).astype(F32).astype(jnp.bfloat16)
    return jnp.concatenate([one, one], 0)


def sweep(e, tiles, coef, adj):
    sub = iota((8, 128), 0)
    flat = jnp.concatenate(e[0] + e[1], 0)
    hi = flat.astype(jnp.bfloat16)
    lo = (flat - hi.astype(F32)).astype(jnp.bfloat16)
    side = jnp.dot(jnp.concatenate([hi, lo], 1), adj, preferred_element_type=F32)
    new = [[], []]
    for f in range(2):
        for t in range(tiles):
            c = e[f][t]
            before = e[f][t - 1] if t else jnp.where(sub == 0, 0.0, roll(e[f][tiles - 1], 1, 0))
            after = e[f][t + 1] if t + 1 < tiles else jnp.where(sub == 7, 0.0, roll(e[f][0], -1, 0))
            at = (f * tiles + t) * 8
            near = before + after + side[at : at + 8]
            new[f].append((1.0 - OMEGA) * c + coef[4 + f, t] + (coef[f, t] * near - coef[2 + f, t] * e[1 - f][t]))
    return new


def sweeps(kind, tiles, u, coef):
    row0 = window_rows(kind, tiles)
    xp, z = lane_ids()
    sub = iota((8, 128), 0)
    adj = adjacency()

    def body(_, flat):
        e = [list(flat[:tiles]), list(flat[tiles:])]
        for _ in range(UNROLL):
            e = sweep(e, tiles, coef, adj)
        return tuple(e[0] + e[1])

    flat = tuple(coef[4 + f, t] for f in range(2) for t in range(tiles))
    for _ in range((SWEEPS - 1) % UNROLL):
        e = sweep([list(flat[:tiles]), list(flat[tiles:])], tiles, coef, adj)
        flat = tuple(e[0] + e[1])
    if SWEEPS - 1 == UNROLL:
        flat = body(0, flat)
    else:
        flat = lax.fori_loop(0, (SWEEPS - 1) // UNROLL, body, flat)
    own_x = (xp >= 4) & (xp < 12)
    for t in range(tiles):
        at = pl.ds(row0 + t, 8, stride=tiles)
        y = row0 - PAD - 128 + sub * tiles + t
        if kind == 0:
            here = own_x & (y >= 0) & (y < 128)
        elif kind == 1:
            here = own_x & (y < 0)
        else:
            here = own_x & (y >= 128)
        for f in range(2):
            u[f, at, :] = u[f, at, :] + jnp.where(here, flat[f * tiles + t], 0.0)


def solve_round(rnd, stat, u, uo, meta, coefs, i, j):
    own = jnp.max(meta[0:8, :])
    left = jnp.max(meta[8:16, :])
    right = jnp.max(meta[16:24, :])
    jobs = [(0, 17, own, coefs[0])]
    if rnd < 5:
        jobs += [(1, WIN[rnd], left, coefs[1]), (2, WIN[rnd], right, coefs[2])]
    for kind, tiles, colour, coef in jobs:
        pl.when(colour == float(rnd))(lambda kind=kind, tiles=tiles, coef=coef: prepare(kind, tiles, stat, u, uo, coef, i, j))
    for kind, tiles, colour, coef in jobs:
        pl.when(colour == float(rnd))(lambda kind=kind, tiles=tiles, coef=coef: sweeps(kind, tiles, u, coef))


def message_items(rnd):
    tiles = (128 + 2 * KEEP[rnd]) // 8
    items = [(f, PAD + 128 - KEEP[rnd] + 8 * q) for f in range(2) for q in range(tiles)]
    third = len(items) // 3
    return [[items[g * third + m] for g in range(3)] for m in range(third)]


def emit(rnd, u, first, second, even):
    xp, _ = lane_ids()

    def write(up, down):
        for m, trio in enumerate(message_items(rnd)):
            tiles = [u[f, pl.ds(row, 8), :] for f, row in trio]
            at = pl.ds(8 * m, 8)
            for ref, lane0 in ((up, 4), (down, 7)):
                a, b, c = (roll(tile, 5 * g - lane0, 1) for g, tile in enumerate(tiles))
                ref[at, :] = jnp.where(xp < 5, a, jnp.where(xp < 10, b, c))

    pl.when(even)(lambda: write(second, first))
    pl.when(jnp.logical_not(even))(lambda: write(first, second))


def absorb(rnd, u, uo, first, second, i):
    xp, _ = lane_ids()
    has_above = (i > 0).astype(F32)
    has_below = (i < NGX - 1).astype(F32)

    def read(above, below):
        for m, trio in enumerate(message_items(rnd)):
            a = above[pl.ds(8 * m, 8), :] * has_above
            b = below[pl.ds(8 * m, 8), :] * has_below
            for g, (f, row) in enumerate(trio):
                at = pl.ds(row, 8)
                inner = jnp.where(xp >= 12, roll(b, 12 - 5 * g, 1), u[f, at, :])
                u[f, at, :] = jnp.where(xp < 4, roll(a, -5 * g - 1, 1), inner)
                uo[f, at, :] = jnp.where(xp == 0, roll(a, -5 * g, 1), roll(b, 11 - 5 * g, 1))

    even = i % 2 == 0
    pl.when(even)(lambda: read(second, first))
    pl.when(jnp.logical_not(even))(lambda: read(first, second))


def start_kernel(own, left, right, first, second, stat, u, meta, fin, out1, out2, near, buf, uo, c0, c1, c2):
    i, j = block_here()
    even = i % 2 == 0

    def place(above, below):
        near[0] = above[...]
        near[1] = below[...]

    pl.when(even)(lambda: place(second, first))
    pl.when(jnp.logical_not(even))(lambda: place(first, second))
    above, below = near.at[0], near.at[1]
    xp, _ = lane_ids()
    lane = iota((8, 128), 1)
    full_lane = iota((128, 128), 1)
    full_xp = full_lane & 15
    gx = i * 8 + full_xp - 4
    in_x = (gx >= 0) & (gx < NGX * 8)
    for n, ref in enumerate((own, left, right)):
        valid = ((j > 0) if n == 1 else (j < NGY - 1)) if n else (j >= 0)
        colour = jnp.where(lane == 32, jnp.where(valid, 1.0, 0.0) * (ref[48] + 1.0), 0.0) - 1.0
        meta[n * 8 : n * 8 + 8, :] = colour
    fin[0] = left[48] * (j > 0).astype(F32)
    fin[1] = right[48] * (j < NGY - 1).astype(F32)
    for f in range(2):
        fin[2 + f] = above[25 + f, :, 128:256] * (i > 0).astype(F32)
        fin[4 + f] = below[25 + f, :, 128:256] * (i < NGX - 1).astype(F32)
    for f in range(2):
        u[f, 0:PAD, :] = jnp.zeros((PAD, 128), F32)
        u[f, ROWS - PAD : ROWS, :] = jnp.zeros((PAD, 128), F32)
    for part, ref in enumerate((left, own, right)):
        lanes = slice(part * 128, part * 128 + 128)
        rows = slice(PAD + part * 128, PAD + part * 128 + 128)
        gy = (j - 1 + part) * 128
        in_y = (gy >= 0) & (gy < NGY * 128)

        def gather(a):
            slot = a % 2
            for p in range(4):
                for h in range(2):
                    z = 2 * p + h
                    buf[slot, z * 16 : z * 16 + 4, :] = above[a * 4 + p, 4 * h : 4 * h + 4, lanes]
                    buf[slot, z * 16 + 4 : z * 16 + 12, :] = ref[a * 8 + z]
                    buf[slot, z * 16 + 12 : z * 16 + 16, :] = below[a * 4 + p, 4 * h : 4 * h + 4, lanes]
            return buf[slot].T

        stat[0, rows, :] = gather(0)
        stat[1, rows, :] = gather(1)
        stat[2, rows, :] = 0.25 * (gather(2) - 0.125)
        force = [gather(3), gather(4)]
        label = gather(5)
        buf[0] = jnp.zeros((128, 128), F32)
        for z in range(8):
            buf[0, z * 16 : z * 16 + 1, :] = above[24, z : z + 1, lanes]
            buf[0, z * 16 + 15 : z * 16 + 16, :] = below[24, z : z + 1, lanes]
        outer = buf[0].T
        y_ok = in_y.astype(F32)
        out_ok = jnp.where(full_xp == 0, (i > 0).astype(F32), (i < NGX - 1).astype(F32)) * y_ok
        for f in range(2):
            hot = (label == f + 1.0).astype(F32) * (in_x.astype(F32) * y_ok)
            u[f, rows, :] = hot
            stat[3 + f, rows, :] = hot + force[f]
            uo[f, rows, :] = (outer == f + 1.0).astype(F32) * out_ok
    solve_round(0, stat, u, uo, meta, (c0, c1, c2), i, j)
    emit(0, u, out1, out2, even)


def middle_kernel(rnd, stat, u_in, meta, first, second, u, out1, out2, uo, c0, c1, c2):
    i, j = block_here()
    u[...] = u_in[...]
    absorb(rnd - 1, u, uo, first, second, i)
    solve_round(rnd, stat, u, uo, meta, (c0, c1, c2), i, j)
    emit(rnd, u, out1, out2, i % 2 == 0)


def last_kernel(stat, u_in, meta, first, second, fin, own, nat, rows, u, uo, c0):
    i, j = block_here()
    u[...] = u_in[...]
    absorb(4, u, uo, first, second, i)
    solve_round(5, stat, u, uo, meta, (c0,), i, j)
    sub = iota((8, 128), 0)
    lane = iota((8, 128), 1)
    tiles = []
    for f in range(2):
        flat = u[f, PAD + 128 : PAD + 256, :].T
        for z in range(8):
            tile = flat[z * 16 + 4 : z * 16 + 12, :]
            nat[f, z] = tile
            tiles.append(tile)
    cols = edge_columns(tiles)
    sums = [jnp.zeros((8, 128), F32) for _ in range(10)]
    left = cols * roll(fin[0], -16, 1)
    right = cols * roll(fin[1], 16, 1)
    for f in range(2):
        acc = jnp.zeros((8, 128), F32)
        for z in range(8):
            c, other = tiles[f * 8 + z], tiles[(1 - f) * 8 + z]
            near = jnp.where(sub == 0, 0.0, roll(c, 1, 0)) + jnp.where(sub == 7, 0.0, roll(c, -1, 0))
            near = near + jnp.where(lane == 0, 0.0, roll(c, 1, 1)) + jnp.where(lane == 127, 0.0, roll(c, -1, 1))
            if z > 0:
                near = near + tiles[f * 8 + z - 1]
            if z < 7:
                near = near + tiles[f * 8 + z + 1]
            s12 = 0.25 * (own[16 + z] - 0.125)
            rhs = (own[40 + z] == f + 1.0).astype(F32) + own[24 + f * 8 + z]
            acc = acc + own[49 + f * 8 + z] * (rhs - ((own[f * 8 + z] + 6.0) * c + s12 * other - near))
        sums[f] = acc
        top = jnp.zeros((8, 128), F32)
        bot = jnp.zeros((8, 128), F32)
        for z in range(8):
            top = jnp.where(sub == z, jnp.broadcast_to(tiles[f * 8 + z][0:1, :], (8, 128)), top)
            bot = jnp.where(sub == z, jnp.broadcast_to(tiles[f * 8 + z][7:8, :], (8, 128)), bot)
        sums[2 + f] = top * fin[2 + f]
        sums[4 + f] = bot * fin[4 + f]
        sums[6 + f] = jnp.where((lane >= f * 8) & (lane < f * 8 + 8), left, 0.0)
        sums[8 + f] = jnp.where((lane >= 16 + f * 8) & (lane < 24 + f * 8), right, 0.0)
    here = i * NGY + j
    slot = iota((2, 128), 0) * 128 + iota((2, 128), 1)
    row = jnp.zeros((2, 128), F32)
    for n, at in enumerate((here, here - NGY, here + NGY, here - 1, here + 1)):
        for f in range(2):
            total = jnp.sum(sums[2 * n + f], keepdims=True) * (1.0 / 8192.0)
            row = jnp.where(slot == 2 * at + f, total, row)
    rows[...] = jnp.broadcast_to(row[None], (NGX * NGY, 2, 128))


def lift_kernel(got, inv, basis, nat, out, coarse):
    q = jnp.sum(got[...], axis=0)
    lane = iota((1, 2), 1)
    pair = jnp.zeros((1, 2), F32)
    for f in range(2):
        c = jnp.sum(q[0:1, :] * inv[0, 0, f : f + 1, 0:128] + q[1:2, :] * inv[0, 0, f : f + 1, 128:256], keepdims=True)
        out[f] = nat[f] + basis[f] * c.reshape(1, 1, 1)
        pair = jnp.where(lane == f, c, pair)
    coarse[0] = pair


def sds(*shape):
    return jax.ShapeDtypeStruct(shape, F32)


def call(kernel, out, scratch=(), **kw):
    return pl.pallas_call(
        kernel,
        out_shape=out,
        scratch_shapes=list(scratch),
        compiler_params=pltpu.CompilerParams(vmem_limit_bytes=48 * 1024 * 1024),
        **kw,
    )


def swap(x, odd):
    return send(x, lambda i, j: (home(i, j), home((((i + odd) ^ 1) - odd) % NGX, j)))


def shards(mixing, forcing, labels, colours, coarse_basis, coarse_inverse):
    coef = lambda t: pltpu.VMEM((6, t, 8, 128), F32)
    block, full = call(
        pack_kernel,
        (sds(49, 8, 128), sds(65, 8, 128)),
        [
            pltpu.VMEM((8, 8, 128), jnp.int32),
            pltpu.SemaphoreType.DMA((8,)),
        ],
        in_specs=[pl.BlockSpec(memory_space=pltpu.HBM)] * 4 + [pl.BlockSpec(memory_space=pltpu.VMEM)],
        name="pack",
    )(
        *(pltpu.with_memory_space_constraint(x, pltpu.HBM) for x in (mixing, forcing, labels, coarse_basis)),
        jnp.broadcast_to(colours, (8, 128)),
    )
    own = send(full, lambda i, j: (i * NGY + j, home(i, j)))
    left = send(block, lambda i, j: (i * NGY + j, home(i, (j + 1) % NGY)))
    right = send(block, lambda i, j: (i * NGY + j, home(i, (j - 1) % NGY)))
    one, two = call(rows_kernel, (sds(27, 8, 384), sds(27, 8, 384)), name="rows")(own, left, right)
    one, two = swap(one, 0), swap(two, 1)
    msg = lambda r: sds(8 * len(message_items(r)), 128)
    stat, u, meta, fin, one, two = call(
        start_kernel,
        (sds(5, ROWS, 128), sds(2, ROWS, 128), sds(24, 128), sds(6, 8, 128), msg(0), msg(0)),
        [pltpu.VMEM((2, 27, 8, 384), F32), pltpu.VMEM((2, 128, 128), F32), pltpu.VMEM((2, ROWS, 128), F32)]
        + [coef(17), coef(16), coef(16)],
        name="round0",
    )(own, left, right, one, two)
    for rnd in range(1, 5):
        one, two = swap(one, 0), swap(two, 1)
        u, one, two = call(
            lambda *refs, rnd=rnd: middle_kernel(rnd, *refs),
            (sds(2, ROWS, 128), msg(rnd), msg(rnd)),
            [pltpu.VMEM((2, ROWS, 128), F32), coef(17), coef(16), coef(16)],
            name=f"round{rnd}",
        )(stat, u, meta, one, two)
    one, two = swap(one, 0), swap(two, 1)
    nat, rows = call(
        last_kernel,
        (sds(2, 8, 8, 128), sds(NGX * NGY, 2, 128)),
        [pltpu.VMEM((2, ROWS, 128), F32), pltpu.VMEM((2, ROWS, 128), F32), coef(17)],
        name="round5",
    )(stat, u, meta, one, two, fin, own)
    nat = send(nat, lambda i, j: (home(i, j), i * NGY + j))
    got = lax.all_to_all(rows, ("gx", "gy"), 0, 0, tiled=True)
    return call(lift_kernel, (sds(2, 8, 8, 128), sds(1, 1, 2)), name="lift")(got, coarse_inverse, coarse_basis, nat)


def solution(mesh):
    return jax.shard_map(
        shards,
        mesh=mesh,
        in_specs=(
            P(None, None, "gx", "gy"),
            P(None, None, "gx", "gy"),
            P(None, "gx", "gy"),
            P("gx", "gy"),
            P(None, None, "gx", "gy"),
            P("gx", "gy", None, None),
        ),
        out_specs=(P(None, None, "gx", "gy"), P("gx", "gy", None)),
        check_vma=False,
    )
```

```python
import jax
import jax.numpy as jnp
from jax import lax
from jax.experimental import pallas as pl
from jax.experimental.pallas import tpu as pltpu
from jax.sharding import PartitionSpec as P

SWEEPS = 20
OMEGA = 0.8
UNROLL = 19
PAD = 8
WIN = (16, 13, 10, 7, 4)
KEEP = (104, 80, 56, 32, 8)
ROWS = 400
F32 = jnp.float32
NGX = 16
NGY = 8


def home(i, j):
    y, a, core = i // 4, i // 2 % 2, i % 2
    low = a if y % 2 == 0 else 1 - a
    return (y * 4 + j // 4 * 2 + core) * NGY + low * 4 + j % 4


def block_here():
    gx, gy = lax.axis_index("gx"), lax.axis_index("gy")
    y, low = gx // 4, gy // 4
    a = jnp.where(y % 2 == 0, low, 1 - low)
    return y * 4 + a * 2 + gx % 2, gx // 2 % 2 * 4 + gy % 4


def send(x, to):
    blocks = [(i, j) for i in range(NGX) for j in range(NGY)]
    return lax.ppermute(x, ("gx", "gy"), [to(i, j) for i, j in blocks])


def iota(shape, dim):
    return lax.broadcasted_iota(jnp.int32, shape, dim)


def roll(x, by, axis):
    by = by % x.shape[axis]
    return x if by == 0 else pltpu.roll(x, by, axis)


def lane_ids():
    lane = iota((8, 128), 1)
    return lane & 15, lane >> 4


def edge_columns(tiles):
    lane = iota((8, 128), 1)
    out = jnp.zeros((8, 128), F32)
    for n, tile in enumerate(tiles):
        out = jnp.where(lane == n, roll(tile, n, 1), out)
        out = jnp.where(lane == 16 + n, roll(tile, 17 + n, 1), out)
    return out


def pack_kernel(mix, forc, lab, basis, colour, out, full, lab_v, sems):
    copies = [
        pltpu.make_async_copy(lab, lab_v, sems.at[0]),
        pltpu.make_async_copy(basis.at[0], full.at[pl.ds(49, 8)], sems.at[1]),
        pltpu.make_async_copy(basis.at[1], full.at[pl.ds(57, 8)], sems.at[2]),
    ]
    for f in range(3):
        copies.append(pltpu.make_async_copy(mix.at[f], out.at[pl.ds(f * 8, 8)], sems.at[3 + f]))
    for f in range(2):
        copies.append(pltpu.make_async_copy(forc.at[f], out.at[pl.ds(24 + f * 8, 8)], sems.at[6 + f]))
    for c in copies:
        c.start()
    for c in copies:
        c.wait()
    out[40:48] = lab_v[...].astype(F32)
    cols = edge_columns([full[49 + n] for n in range(16)])
    lane = iota((8, 128), 1)
    out[48] = jnp.where(lane == 32, colour[...].astype(F32), cols)
    full[0:49] = out[...]


def rows_kernel(own, left, right, first, second):
    even = block_here()[0] % 2 == 0
    pl.when(even)(lambda: write_rows(own, left, right, second, first))
    pl.when(jnp.logical_not(even))(lambda: write_rows(own, left, right, first, second))


def write_rows(own, left, right, up, down):
    for part, ref in enumerate((left, own, right)):
        lanes = slice(part * 128, part * 128 + 128)
        for a in range(6):
            for p in range(4):
                lo, hi = ref[a * 8 + 2 * p], ref[a * 8 + 2 * p + 1]
                sub = iota((8, 128), 0)
                up[a * 4 + p, :, lanes] = jnp.where(sub < 4, lo, roll(hi, 4, 0))
                down[a * 4 + p, :, lanes] = jnp.where(sub < 4, roll(lo, 4, 0), hi)
        for z in range(8):
            up[24, z : z + 1, lanes] = ref[40 + z, 4:5, :]
            down[24, z : z + 1, lanes] = ref[40 + z, 3:4, :]
            for f in range(2):
                if part == 1:
                    up[25 + f, z : z + 1, lanes] = own[49 + f * 8 + z, 0:1, :]
                    down[25 + f, z : z + 1, lanes] = own[49 + f * 8 + z, 7:8, :]
        if part != 1:
            up[25:27, :, lanes] = jnp.zeros((2, 8, 128), F32)
            down[25:27, :, lanes] = jnp.zeros((2, 8, 128), F32)


def window_rows(kind, tiles):
    if kind == 0:
        return PAD + 128 - 4
    if kind == 1:
        return PAD + 128 + 4 - 8 * tiles
    return PAD + 128 + 124


def prepare(kind, tiles, stat, u, uo, coef, i, j):
    row0 = window_rows(kind, tiles)
    xp, z = lane_ids()
    sub = iota((8, 128), 0)
    rim_x = ((xp == 0) | (xp == 15)).astype(F32)
    gx = i * 8 + xp - 4
    in_x = ((gx >= 0) & (gx < NGX * 8)).astype(F32)
    for t in range(tiles):
        at = pl.ds(row0 + t, 8, stride=tiles)
        s11, s22, s12 = stat[0, at, :], stat[1, at, :], stat[2, at, :]
        y = row0 - PAD - 128 + sub * tiles + t + j * 128
        inside = in_x * ((y >= 0) & (y < NGY * 128)).astype(F32)
        diag = 6.0 + rim_x
        if t == 0 and kind != 1:
            diag = diag + (sub == 0).astype(F32)
        if t == tiles - 1 and kind != 2:
            diag = diag + (sub == 7).astype(F32)
        vals = []
        for f in range(2):
            c = u[f, at, :]
            near = u[f, pl.ds(row0 + t - 1, 8, stride=tiles), :] + u[f, pl.ds(row0 + t + 1, 8, stride=tiles), :]
            out = uo[f, at, :]
            near = near + jnp.where(xp == 0, out, roll(c, 1, 1)) + jnp.where(xp == 15, out, roll(c, -1, 1))
            near = near + jnp.where(z == 0, 0.0, roll(c, 16, 1)) + jnp.where(z == 7, 0.0, roll(c, -16, 1))
            vals.append((c, near))
        for f, s in ((0, s11), (1, s22)):
            c, near = vals[f]
            r = stat[3 + f, at, :] - ((s + 6.0) * c + s12 * vals[1 - f][0] - near)
            w = OMEGA * inside / (s + diag)
            coef[f, t] = w
            coef[2 + f, t] = w * s12
            coef[4 + f, t] = w * r


def adjacency():
    a, b = iota((128, 128), 0), iota((128, 128), 1)
    ax, az, bx, bz = a & 15, a >> 4, b & 15, b >> 4
    near_x = (az == bz) & ((ax - bx == 1) | (bx - ax == 1))
    near_z = (ax == bx) & ((az - bz == 1) | (bz - az == 1))
    one = (near_x | near_z).astype(F32).astype(jnp.bfloat16)
    return jnp.concatenate([one, one], 0)


def sweep(e, tiles, coef, adj):
    sub = iota((8, 128), 0)
    flat = jnp.concatenate(e[0] + e[1], 0)
    hi = flat.astype(jnp.bfloat16)
    lo = (flat - hi.astype(F32)).astype(jnp.bfloat16)
    side = jnp.dot(jnp.concatenate([hi, lo], 1), adj, preferred_element_type=F32)
    new = [[], []]
    for f in range(2):
        for t in range(tiles):
            c = e[f][t]
            before = e[f][t - 1] if t else jnp.where(sub == 0, 0.0, roll(e[f][tiles - 1], 1, 0))
            after = e[f][t + 1] if t + 1 < tiles else jnp.where(sub == 7, 0.0, roll(e[f][0], -1, 0))
            at = (f * tiles + t) * 8
            near = before + after + side[at : at + 8]
            new[f].append((1.0 - OMEGA) * c + coef[4 + f, t] + (coef[f, t] * near - coef[2 + f, t] * e[1 - f][t]))
    return new


def sweeps(kind, tiles, u, coef):
    row0 = window_rows(kind, tiles)
    xp, z = lane_ids()
    sub = iota((8, 128), 0)
    adj = adjacency()

    def body(_, flat):
        e = [list(flat[:tiles]), list(flat[tiles:])]
        for _ in range(UNROLL):
            e = sweep(e, tiles, coef, adj)
        return tuple(e[0] + e[1])

    flat = tuple(coef[4 + f, t] for f in range(2) for t in range(tiles))
    for _ in range((SWEEPS - 1) % UNROLL):
        e = sweep([list(flat[:tiles]), list(flat[tiles:])], tiles, coef, adj)
        flat = tuple(e[0] + e[1])
    if SWEEPS - 1 == UNROLL:
        flat = body(0, flat)
    else:
        flat = lax.fori_loop(0, (SWEEPS - 1) // UNROLL, body, flat)
    own_x = (xp >= 4) & (xp < 12)
    for t in range(tiles):
        at = pl.ds(row0 + t, 8, stride=tiles)
        y = row0 - PAD - 128 + sub * tiles + t
        if kind == 0:
            here = own_x & (y >= 0) & (y < 128)
        elif kind == 1:
            here = own_x & (y < 0)
        else:
            here = own_x & (y >= 128)
        for f in range(2):
            u[f, at, :] = u[f, at, :] + jnp.where(here, flat[f * tiles + t], 0.0)


def solve_round(rnd, stat, u, uo, meta, coefs, i, j):
    own = jnp.max(meta[0:8, :])
    left = jnp.max(meta[8:16, :])
    right = jnp.max(meta[16:24, :])
    jobs = [(0, 17, own, coefs[0])]
    if rnd < 5:
        jobs += [(1, WIN[rnd], left, coefs[1]), (2, WIN[rnd], right, coefs[2])]
    for kind, tiles, colour, coef in jobs:
        pl.when(colour == float(rnd))(lambda kind=kind, tiles=tiles, coef=coef: prepare(kind, tiles, stat, u, uo, coef, i, j))
    for kind, tiles, colour, coef in jobs:
        pl.when(colour == float(rnd))(lambda kind=kind, tiles=tiles, coef=coef: sweeps(kind, tiles, u, coef))


def message_items(rnd):
    tiles = (128 + 2 * KEEP[rnd]) // 8
    items = [(f, PAD + 128 - KEEP[rnd] + 8 * q) for f in range(2) for q in range(tiles)]
    third = len(items) // 3
    return [[items[g * third + m] for g in range(3)] for m in range(third)]


def emit(rnd, u, first, second, even):
    xp, _ = lane_ids()

    def write(up, down):
        for m, trio in enumerate(message_items(rnd)):
            tiles = [u[f, pl.ds(row, 8), :] for f, row in trio]
            at = pl.ds(8 * m, 8)
            for ref, lane0 in ((up, 4), (down, 7)):
                a, b, c = (roll(tile, 5 * g - lane0, 1) for g, tile in enumerate(tiles))
                ref[at, :] = jnp.where(xp < 5, a, jnp.where(xp < 10, b, c))

    pl.when(even)(lambda: write(second, first))
    pl.when(jnp.logical_not(even))(lambda: write(first, second))


def absorb(rnd, u, uo, first, second, i):
    xp, _ = lane_ids()
    has_above = (i > 0).astype(F32)
    has_below = (i < NGX - 1).astype(F32)

    def read(above, below):
        for m, trio in enumerate(message_items(rnd)):
            a = above[pl.ds(8 * m, 8), :] * has_above
            b = below[pl.ds(8 * m, 8), :] * has_below
            for g, (f, row) in enumerate(trio):
                at = pl.ds(row, 8)
                inner = jnp.where(xp >= 12, roll(b, 12 - 5 * g, 1), u[f, at, :])
                u[f, at, :] = jnp.where(xp < 4, roll(a, -5 * g - 1, 1), inner)
                uo[f, at, :] = jnp.where(xp == 0, roll(a, -5 * g, 1), roll(b, 11 - 5 * g, 1))

    even = i % 2 == 0
    pl.when(even)(lambda: read(second, first))
    pl.when(jnp.logical_not(even))(lambda: read(first, second))


def start_kernel(own, left, right, first, second, stat, u, meta, fin, out1, out2, near, buf, uo, c0, c1, c2):
    i, j = block_here()
    even = i % 2 == 0

    def place(above, below):
        near[0] = above[...]
        near[1] = below[...]

    pl.when(even)(lambda: place(second, first))
    pl.when(jnp.logical_not(even))(lambda: place(first, second))
    above, below = near.at[0], near.at[1]
    xp, _ = lane_ids()
    lane = iota((8, 128), 1)
    full_lane = iota((128, 128), 1)
    full_xp = full_lane & 15
    gx = i * 8 + full_xp - 4
    in_x = (gx >= 0) & (gx < NGX * 8)
    for n, ref in enumerate((own, left, right)):
        valid = ((j > 0) if n == 1 else (j < NGY - 1)) if n else (j >= 0)
        colour = jnp.where(lane == 32, jnp.where(valid, 1.0, 0.0) * (ref[48] + 1.0), 0.0) - 1.0
        meta[n * 8 : n * 8 + 8, :] = colour
    fin[0] = left[48] * (j > 0).astype(F32)
    fin[1] = right[48] * (j < NGY - 1).astype(F32)
    for f in range(2):
        fin[2 + f] = above[25 + f, :, 128:256] * (i > 0).astype(F32)
        fin[4 + f] = below[25 + f, :, 128:256] * (i < NGX - 1).astype(F32)
    for f in range(2):
        u[f, 0:PAD, :] = jnp.zeros((PAD, 128), F32)
        u[f, ROWS - PAD : ROWS, :] = jnp.zeros((PAD, 128), F32)
    for part, ref in enumerate((left, own, right)):
        lanes = slice(part * 128, part * 128 + 128)
        rows = slice(PAD + part * 128, PAD + part * 128 + 128)
        gy = (j - 1 + part) * 128
        in_y = (gy >= 0) & (gy < NGY * 128)

        def gather(a):
            slot = a % 2
            for p in range(4):
                for h in range(2):
                    z = 2 * p + h
                    buf[slot, z * 16 : z * 16 + 4, :] = above[a * 4 + p, 4 * h : 4 * h + 4, lanes]
                    buf[slot, z * 16 + 4 : z * 16 + 12, :] = ref[a * 8 + z]
                    buf[slot, z * 16 + 12 : z * 16 + 16, :] = below[a * 4 + p, 4 * h : 4 * h + 4, lanes]
            return buf[slot].T

        stat[0, rows, :] = gather(0)
        stat[1, rows, :] = gather(1)
        stat[2, rows, :] = 0.25 * (gather(2) - 0.125)
        force = [gather(3), gather(4)]
        label = gather(5)
        buf[0] = jnp.zeros((128, 128), F32)
        for z in range(8):
            buf[0, z * 16 : z * 16 + 1, :] = above[24, z : z + 1, lanes]
            buf[0, z * 16 + 15 : z * 16 + 16, :] = below[24, z : z + 1, lanes]
        outer = buf[0].T
        y_ok = in_y.astype(F32)
        out_ok = jnp.where(full_xp == 0, (i > 0).astype(F32), (i < NGX - 1).astype(F32)) * y_ok
        for f in range(2):
            hot = (label == f + 1.0).astype(F32) * (in_x.astype(F32) * y_ok)
            u[f, rows, :] = hot
            stat[3 + f, rows, :] = hot + force[f]
            uo[f, rows, :] = (outer == f + 1.0).astype(F32) * out_ok
    solve_round(0, stat, u, uo, meta, (c0, c1, c2), i, j)
    emit(0, u, out1, out2, even)


def middle_kernel(rnd, stat, u_in, meta, first, second, u, out1, out2, uo, c0, c1, c2):
    i, j = block_here()
    u[...] = u_in[...]
    absorb(rnd - 1, u, uo, first, second, i)
    solve_round(rnd, stat, u, uo, meta, (c0, c1, c2), i, j)
    emit(rnd, u, out1, out2, i % 2 == 0)


def last_kernel(stat, u_in, meta, first, second, nat, u, uo, c0):
    i, j = block_here()
    u[...] = u_in[...]
    absorb(4, u, uo, first, second, i)
    solve_round(5, stat, u, uo, meta, (c0,), i, j)
    for f in range(2):
        flat = u[f, PAD + 128 : PAD + 256, :].T
        for z in range(8):
            nat[f, z] = flat[z * 16 + 4 : z * 16 + 12, :]


def coarse_kernel(nat, own, fin, rows):
    i, j = block_here()
    sub = iota((8, 128), 0)
    lane = iota((8, 128), 1)
    tiles = [nat[f, z] for f in range(2) for z in range(8)]
    cols = edge_columns(tiles)
    sums = [jnp.zeros((8, 128), F32) for _ in range(10)]
    left = cols * roll(fin[0], -16, 1)
    right = cols * roll(fin[1], 16, 1)
    for f in range(2):
        acc = jnp.zeros((8, 128), F32)
        for z in range(8):
            c, other = tiles[f * 8 + z], tiles[(1 - f) * 8 + z]
            near = jnp.where(sub == 0, 0.0, roll(c, 1, 0)) + jnp.where(sub == 7, 0.0, roll(c, -1, 0))
            near = near + jnp.where(lane == 0, 0.0, roll(c, 1, 1)) + jnp.where(lane == 127, 0.0, roll(c, -1, 1))
            if z > 0:
                near = near + tiles[f * 8 + z - 1]
            if z < 7:
                near = near + tiles[f * 8 + z + 1]
            s12 = 0.25 * (own[16 + z] - 0.125)
            rhs = (own[40 + z] == f + 1.0).astype(F32) + own[24 + f * 8 + z]
            acc = acc + own[49 + f * 8 + z] * (rhs - ((own[f * 8 + z] + 6.0) * c + s12 * other - near))
        sums[f] = acc
        top = jnp.zeros((8, 128), F32)
        bot = jnp.zeros((8, 128), F32)
        for z in range(8):
            top = jnp.where(sub == z, jnp.broadcast_to(tiles[f * 8 + z][0:1, :], (8, 128)), top)
            bot = jnp.where(sub == z, jnp.broadcast_to(tiles[f * 8 + z][7:8, :], (8, 128)), bot)
        sums[2 + f] = top * fin[2 + f]
        sums[4 + f] = bot * fin[4 + f]
        sums[6 + f] = jnp.where((lane >= f * 8) & (lane < f * 8 + 8), left, 0.0)
        sums[8 + f] = jnp.where((lane >= 16 + f * 8) & (lane < 24 + f * 8), right, 0.0)
    here = i * NGY + j
    slot = iota((2, 128), 0) * 128 + iota((2, 128), 1)
    row = jnp.zeros((2, 128), F32)
    for n, at in enumerate((here, here - NGY, here + NGY, here - 1, here + 1)):
        for f in range(2):
            total = jnp.sum(sums[2 * n + f], keepdims=True) * (1.0 / 8192.0)
            row = jnp.where(slot == 2 * at + f, total, row)
    rows[...] = jnp.broadcast_to(row[None], (NGX * NGY, 2, 128))


def lift_kernel(got, inv, basis, nat, out, coarse):
    q = jnp.sum(got[...], axis=0)
    lane = iota((1, 2), 1)
    pair = jnp.zeros((1, 2), F32)
    for f in range(2):
        c = jnp.sum(q[0:1, :] * inv[0, 0, f : f + 1, 0:128] + q[1:2, :] * inv[0, 0, f : f + 1, 128:256], keepdims=True)
        out[f] = nat[f] + basis[f] * c.reshape(1, 1, 1)
        pair = jnp.where(lane == f, c, pair)
    coarse[0] = pair


def sds(*shape):
    return jax.ShapeDtypeStruct(shape, F32)


def call(kernel, out, scratch=(), **kw):
    return pl.pallas_call(
        kernel,
        out_shape=out,
        scratch_shapes=list(scratch),
        compiler_params=pltpu.CompilerParams(vmem_limit_bytes=48 * 1024 * 1024),
        **kw,
    )


def swap(x, odd):
    return send(x, lambda i, j: (home(i, j), home((((i + odd) ^ 1) - odd) % NGX, j)))


def shards(mixing, forcing, labels, colours, coarse_basis, coarse_inverse):
    coef = lambda t: pltpu.VMEM((6, t, 8, 128), F32)
    block, full = call(
        pack_kernel,
        (sds(49, 8, 128), sds(65, 8, 128)),
        [
            pltpu.VMEM((8, 8, 128), jnp.int32),
            pltpu.SemaphoreType.DMA((8,)),
        ],
        in_specs=[pl.BlockSpec(memory_space=pltpu.HBM)] * 4 + [pl.BlockSpec(memory_space=pltpu.VMEM)],
        name="pack",
    )(
        *(pltpu.with_memory_space_constraint(x, pltpu.HBM) for x in (mixing, forcing, labels, coarse_basis)),
        jnp.broadcast_to(colours, (8, 128)),
    )
    own = send(full, lambda i, j: (i * NGY + j, home(i, j)))
    left = send(block, lambda i, j: (i * NGY + j, home(i, (j + 1) % NGY)))
    right = send(block, lambda i, j: (i * NGY + j, home(i, (j - 1) % NGY)))
    one, two = call(rows_kernel, (sds(27, 8, 384), sds(27, 8, 384)), name="rows")(own, left, right)
    one, two = swap(one, 0), swap(two, 1)
    msg = lambda r: sds(8 * len(message_items(r)), 128)
    stat, u, meta, fin, one, two = call(
        start_kernel,
        (sds(5, ROWS, 128), sds(2, ROWS, 128), sds(24, 128), sds(6, 8, 128), msg(0), msg(0)),
        [pltpu.VMEM((2, 27, 8, 384), F32), pltpu.VMEM((2, 128, 128), F32), pltpu.VMEM((2, ROWS, 128), F32)]
        + [coef(17), coef(16), coef(16)],
        name="round0",
    )(own, left, right, one, two)
    for rnd in range(1, 5):
        one, two = swap(one, 0), swap(two, 1)
        u, one, two = call(
            lambda *refs, rnd=rnd: middle_kernel(rnd, *refs),
            (sds(2, ROWS, 128), msg(rnd), msg(rnd)),
            [pltpu.VMEM((2, ROWS, 128), F32), coef(17), coef(16), coef(16)],
            name=f"round{rnd}",
        )(stat, u, meta, one, two)
    one, two = swap(one, 0), swap(two, 1)
    nat = call(
        last_kernel,
        sds(2, 8, 8, 128),
        [pltpu.VMEM((2, ROWS, 128), F32), pltpu.VMEM((2, ROWS, 128), F32), coef(17)],
        name="round5",
    )(stat, u, meta, one, two)
    back = send(nat, lambda i, j: (home(i, j), i * NGY + j))
    rows = call(coarse_kernel, sds(NGX * NGY, 2, 128), name="coarse")(nat, own, fin)
    got = lax.all_to_all(rows, ("gx", "gy"), 0, 0, tiled=True)
    return call(lift_kernel, (sds(2, 8, 8, 128), sds(1, 1, 2)), name="lift")(got, coarse_inverse, coarse_basis, back)


def solution(mesh):
    return jax.shard_map(
        shards,
        mesh=mesh,
        in_specs=(
            P(None, None, "gx", "gy"),
            P(None, None, "gx", "gy"),
            P(None, "gx", "gy"),
            P("gx", "gy"),
            P(None, None, "gx", "gy"),
            P("gx", "gy", None, None),
        ),
        out_specs=(P(None, None, "gx", "gy"), P("gx", "gy", None)),
        check_vma=False,
    )
```

```python
import jax
import jax.numpy as jnp
from jax import lax
from jax.experimental import pallas as pl
from jax.experimental.pallas import tpu as pltpu
from jax.sharding import PartitionSpec as P

SWEEPS = 20
OMEGA = 0.8
UNROLL = 6
PAD = 8
WIN = (16, 13, 10, 7, 4)
KEEP = (104, 80, 56, 32, 8)
ROWS = 400
F32 = jnp.float32
NGX = 16
NGY = 8


def home(i, j):
    y, a, core = i // 4, i // 2 % 2, i % 2
    low = a if y % 2 == 0 else 1 - a
    return (y * 4 + j // 4 * 2 + core) * NGY + low * 4 + j % 4


def block_here():
    gx, gy = lax.axis_index("gx"), lax.axis_index("gy")
    y, low = gx // 4, gy // 4
    a = jnp.where(y % 2 == 0, low, 1 - low)
    return y * 4 + a * 2 + gx % 2, gx // 2 % 2 * 4 + gy % 4


def send(x, to):
    blocks = [(i, j) for i in range(NGX) for j in range(NGY)]
    return lax.ppermute(x, ("gx", "gy"), [to(i, j) for i, j in blocks])


def iota(shape, dim):
    return lax.broadcasted_iota(jnp.int32, shape, dim)


def roll(x, by, axis):
    by = by % x.shape[axis]
    return x if by == 0 else pltpu.roll(x, by, axis)


def lane_ids():
    lane = iota((8, 128), 1)
    return lane & 15, lane >> 4


def edge_columns(tiles):
    lane = iota((8, 128), 1)
    out = jnp.zeros((8, 128), F32)
    for n, tile in enumerate(tiles):
        out = jnp.where(lane == n, roll(tile, n, 1), out)
        out = jnp.where(lane == 16 + n, roll(tile, 17 + n, 1), out)
    return out


def pack_kernel(mix, forc, lab, basis, colour, out, full, lab_v, sems):
    copies = [
        pltpu.make_async_copy(lab, lab_v, sems.at[0]),
        pltpu.make_async_copy(basis.at[0], full.at[pl.ds(49, 8)], sems.at[1]),
        pltpu.make_async_copy(basis.at[1], full.at[pl.ds(57, 8)], sems.at[2]),
    ]
    for f in range(3):
        copies.append(pltpu.make_async_copy(mix.at[f], out.at[pl.ds(f * 8, 8)], sems.at[3 + f]))
    for f in range(2):
        copies.append(pltpu.make_async_copy(forc.at[f], out.at[pl.ds(24 + f * 8, 8)], sems.at[6 + f]))
    for c in copies:
        c.start()
    for c in copies:
        c.wait()
    out[40:48] = lab_v[...].astype(F32)
    cols = edge_columns([full[49 + n] for n in range(16)])
    lane = iota((8, 128), 1)
    out[48] = jnp.where(lane == 32, colour[...].astype(F32), cols)
    full[0:49] = out[...]


def rows_kernel(own, left, right, first, second):
    even = block_here()[0] % 2 == 0
    pl.when(even)(lambda: write_rows(own, left, right, second, first))
    pl.when(jnp.logical_not(even))(lambda: write_rows(own, left, right, first, second))


def write_rows(own, left, right, up, down):
    for part, ref in enumerate((left, own, right)):
        lanes = slice(part * 128, part * 128 + 128)
        for a in range(6):
            for p in range(4):
                lo, hi = ref[a * 8 + 2 * p], ref[a * 8 + 2 * p + 1]
                sub = iota((8, 128), 0)
                up[a * 4 + p, :, lanes] = jnp.where(sub < 4, lo, roll(hi, 4, 0))
                down[a * 4 + p, :, lanes] = jnp.where(sub < 4, roll(lo, 4, 0), hi)
        for z in range(8):
            up[24, z : z + 1, lanes] = ref[40 + z, 4:5, :]
            down[24, z : z + 1, lanes] = ref[40 + z, 3:4, :]
            for f in range(2):
                if part == 1:
                    up[25 + f, z : z + 1, lanes] = own[49 + f * 8 + z, 0:1, :]
                    down[25 + f, z : z + 1, lanes] = own[49 + f * 8 + z, 7:8, :]
        if part != 1:
            up[25:27, :, lanes] = jnp.zeros((2, 8, 128), F32)
            down[25:27, :, lanes] = jnp.zeros((2, 8, 128), F32)


def window_rows(kind, tiles):
    if kind == 0:
        return PAD + 128 - 4
    if kind == 1:
        return PAD + 128 + 4 - 8 * tiles
    return PAD + 128 + 124


def prepare(kind, tiles, stat, u, uo, coef, i, j):
    row0 = window_rows(kind, tiles)
    xp, z = lane_ids()
    sub = iota((8, 128), 0)
    rim_x = ((xp == 0) | (xp == 15)).astype(F32)
    gx = i * 8 + xp - 4
    in_x = ((gx >= 0) & (gx < NGX * 8)).astype(F32)
    for t in range(tiles):
        at = pl.ds(row0 + t, 8, stride=tiles)
        s11, s22, s12 = stat[0, at, :], stat[1, at, :], stat[2, at, :]
        y = row0 - PAD - 128 + sub * tiles + t + j * 128
        inside = in_x * ((y >= 0) & (y < NGY * 128)).astype(F32)
        diag = 6.0 + rim_x
        if t == 0 and kind != 1:
            diag = diag + (sub == 0).astype(F32)
        if t == tiles - 1 and kind != 2:
            diag = diag + (sub == 7).astype(F32)
        vals = []
        for f in range(2):
            c = u[f, at, :]
            near = u[f, pl.ds(row0 + t - 1, 8, stride=tiles), :] + u[f, pl.ds(row0 + t + 1, 8, stride=tiles), :]
            out = uo[f, at, :]
            near = near + jnp.where(xp == 0, out, roll(c, 1, 1)) + jnp.where(xp == 15, out, roll(c, -1, 1))
            near = near + jnp.where(z == 0, 0.0, roll(c, 16, 1)) + jnp.where(z == 7, 0.0, roll(c, -16, 1))
            vals.append((c, near))
        for f, s in ((0, s11), (1, s22)):
            c, near = vals[f]
            r = stat[3 + f, at, :] - ((s + 6.0) * c + s12 * vals[1 - f][0] - near)
            w = OMEGA * inside / (s + diag)
            coef[f, t] = w
            coef[2 + f, t] = w * s12
            coef[4 + f, t] = w * r


def adjacency():
    a, b = iota((128, 128), 0), iota((128, 128), 1)
    ax, az, bx, bz = a & 15, a >> 4, b & 15, b >> 4
    near_x = (az == bz) & ((ax - bx == 1) | (bx - ax == 1))
    near_z = (ax == bx) & ((az - bz == 1) | (bz - az == 1))
    one = (near_x | near_z).astype(F32).astype(jnp.bfloat16)
    return jnp.concatenate([one, one], 0)


def sweep(e, tiles, coef, adj):
    sub = iota((8, 128), 0)
    flat = jnp.concatenate(e[0] + e[1], 0)
    hi = flat.astype(jnp.bfloat16)
    lo = (flat - hi.astype(F32)).astype(jnp.bfloat16)
    side = jnp.dot(jnp.concatenate([hi, lo], 1), adj, preferred_element_type=F32)
    new = [[], []]
    for f in range(2):
        for t in range(tiles):
            c = e[f][t]
            before = e[f][t - 1] if t else jnp.where(sub == 0, 0.0, roll(e[f][tiles - 1], 1, 0))
            after = e[f][t + 1] if t + 1 < tiles else jnp.where(sub == 7, 0.0, roll(e[f][0], -1, 0))
            at = (f * tiles + t) * 8
            near = before + after + side[at : at + 8]
            new[f].append((1.0 - OMEGA) * c + coef[4 + f, t] + (coef[f, t] * near - coef[2 + f, t] * e[1 - f][t]))
    return new


def sweeps(kind, tiles, u, coef):
    row0 = window_rows(kind, tiles)
    xp, z = lane_ids()
    sub = iota((8, 128), 0)
    adj = adjacency()

    def body(_, flat):
        e = [list(flat[:tiles]), list(flat[tiles:])]
        for _ in range(UNROLL):
            e = sweep(e, tiles, coef, adj)
        return tuple(e[0] + e[1])

    flat = tuple(coef[4 + f, t] for f in range(2) for t in range(tiles))
    for _ in range((SWEEPS - 1) % UNROLL):
        e = sweep([list(flat[:tiles]), list(flat[tiles:])], tiles, coef, adj)
        flat = tuple(e[0] + e[1])
    if SWEEPS - 1 == UNROLL:
        flat = body(0, flat)
    else:
        flat = lax.fori_loop(0, (SWEEPS - 1) // UNROLL, body, flat)
    own_x = (xp >= 4) & (xp < 12)
    for t in range(tiles):
        at = pl.ds(row0 + t, 8, stride=tiles)
        y = row0 - PAD - 128 + sub * tiles + t
        if kind == 0:
            here = own_x & (y >= 0) & (y < 128)
        elif kind == 1:
            here = own_x & (y < 0)
        else:
            here = own_x & (y >= 128)
        for f in range(2):
            u[f, at, :] = u[f, at, :] + jnp.where(here, flat[f * tiles + t], 0.0)


def solve_round(rnd, stat, u, uo, meta, coefs, i, j):
    own = jnp.max(meta[0:8, :])
    left = jnp.max(meta[8:16, :])
    right = jnp.max(meta[16:24, :])
    jobs = [(0, 17, own, coefs[0])]
    if rnd < 5:
        jobs += [(1, WIN[rnd], left, coefs[1]), (2, WIN[rnd], right, coefs[2])]
    for kind, tiles, colour, coef in jobs:
        pl.when(colour == float(rnd))(lambda kind=kind, tiles=tiles, coef=coef: prepare(kind, tiles, stat, u, uo, coef, i, j))
    for kind, tiles, colour, coef in jobs:
        pl.when(colour == float(rnd))(lambda kind=kind, tiles=tiles, coef=coef: sweeps(kind, tiles, u, coef))


def message_items(rnd):
    tiles = (128 + 2 * KEEP[rnd]) // 8
    items = [(f, PAD + 128 - KEEP[rnd] + 8 * q) for f in range(2) for q in range(tiles)]
    third = len(items) // 3
    return [[items[g * third + m] for g in range(3)] for m in range(third)]


def emit(rnd, u, first, second, even):
    xp, _ = lane_ids()

    def write(up, down):
        for m, trio in enumerate(message_items(rnd)):
            tiles = [u[f, pl.ds(row, 8), :] for f, row in trio]
            at = pl.ds(8 * m, 8)
            for ref, lane0 in ((up, 4), (down, 7)):
                a, b, c = (roll(tile, 5 * g - lane0, 1) for g, tile in enumerate(tiles))
                ref[at, :] = jnp.where(xp < 5, a, jnp.where(xp < 10, b, c))

    pl.when(even)(lambda: write(second, first))
    pl.when(jnp.logical_not(even))(lambda: write(first, second))


def absorb(rnd, u, uo, first, second, i):
    xp, _ = lane_ids()
    has_above = (i > 0).astype(F32)
    has_below = (i < NGX - 1).astype(F32)

    def read(above, below):
        for m, trio in enumerate(message_items(rnd)):
            a = above[pl.ds(8 * m, 8), :] * has_above
            b = below[pl.ds(8 * m, 8), :] * has_below
            for g, (f, row) in enumerate(trio):
                at = pl.ds(row, 8)
                inner = jnp.where(xp >= 12, roll(b, 12 - 5 * g, 1), u[f, at, :])
                u[f, at, :] = jnp.where(xp < 4, roll(a, -5 * g - 1, 1), inner)
                uo[f, at, :] = jnp.where(xp == 0, roll(a, -5 * g, 1), roll(b, 11 - 5 * g, 1))

    even = i % 2 == 0
    pl.when(even)(lambda: read(second, first))
    pl.when(jnp.logical_not(even))(lambda: read(first, second))


def start_kernel(own, left, right, first, second, stat, u, meta, fin, out1, out2, near, buf, uo, c0, c1, c2):
    i, j = block_here()
    even = i % 2 == 0

    def place(above, below):
        near[0] = above[...]
        near[1] = below[...]

    pl.when(even)(lambda: place(second, first))
    pl.when(jnp.logical_not(even))(lambda: place(first, second))
    above, below = near.at[0], near.at[1]
    xp, _ = lane_ids()
    lane = iota((8, 128), 1)
    full_lane = iota((128, 128), 1)
    full_xp = full_lane & 15
    gx = i * 8 + full_xp - 4
    in_x = (gx >= 0) & (gx < NGX * 8)
    for n, ref in enumerate((own, left, right)):
        valid = ((j > 0) if n == 1 else (j < NGY - 1)) if n else (j >= 0)
        colour = jnp.where(lane == 32, jnp.where(valid, 1.0, 0.0) * (ref[48] + 1.0), 0.0) - 1.0
        meta[n * 8 : n * 8 + 8, :] = colour
    fin[0] = left[48] * (j > 0).astype(F32)
    fin[1] = right[48] * (j < NGY - 1).astype(F32)
    for f in range(2):
        fin[2 + f] = above[25 + f, :, 128:256] * (i > 0).astype(F32)
        fin[4 + f] = below[25 + f, :, 128:256] * (i < NGX - 1).astype(F32)
    for f in range(2):
        u[f, 0:PAD, :] = jnp.zeros((PAD, 128), F32)
        u[f, ROWS - PAD : ROWS, :] = jnp.zeros((PAD, 128), F32)
    for part, ref in enumerate((left, own, right)):
        lanes = slice(part * 128, part * 128 + 128)
        rows = slice(PAD + part * 128, PAD + part * 128 + 128)
        gy = (j - 1 + part) * 128
        in_y = (gy >= 0) & (gy < NGY * 128)

        def gather(a):
            slot = a % 2
            for p in range(4):
                for h in range(2):
                    z = 2 * p + h
                    buf[slot, z * 16 : z * 16 + 4, :] = above[a * 4 + p, 4 * h : 4 * h + 4, lanes]
                    buf[slot, z * 16 + 4 : z * 16 + 12, :] = ref[a * 8 + z]
                    buf[slot, z * 16 + 12 : z * 16 + 16, :] = below[a * 4 + p, 4 * h : 4 * h + 4, lanes]
            return buf[slot].T

        stat[0, rows, :] = gather(0)
        stat[1, rows, :] = gather(1)
        stat[2, rows, :] = 0.25 * (gather(2) - 0.125)
        force = [gather(3), gather(4)]
        label = gather(5)
        buf[0] = jnp.zeros((128, 128), F32)
        for z in range(8):
            buf[0, z * 16 : z * 16 + 1, :] = above[24, z : z + 1, lanes]
            buf[0, z * 16 + 15 : z * 16 + 16, :] = below[24, z : z + 1, lanes]
        outer = buf[0].T
        y_ok = in_y.astype(F32)
        out_ok = jnp.where(full_xp == 0, (i > 0).astype(F32), (i < NGX - 1).astype(F32)) * y_ok
        for f in range(2):
            hot = (label == f + 1.0).astype(F32) * (in_x.astype(F32) * y_ok)
            u[f, rows, :] = hot
            stat[3 + f, rows, :] = hot + force[f]
            uo[f, rows, :] = (outer == f + 1.0).astype(F32) * out_ok
    solve_round(0, stat, u, uo, meta, (c0, c1, c2), i, j)
    emit(0, u, out1, out2, even)


def middle_kernel(rnd, stat, u_in, meta, first, second, u, out1, out2, uo, c0, c1, c2):
    i, j = block_here()
    u[...] = u_in[...]
    absorb(rnd - 1, u, uo, first, second, i)
    solve_round(rnd, stat, u, uo, meta, (c0, c1, c2), i, j)
    emit(rnd, u, out1, out2, i % 2 == 0)


def last_kernel(stat, u_in, meta, first, second, nat, u, uo, c0):
    i, j = block_here()
    u[...] = u_in[...]
    absorb(4, u, uo, first, second, i)
    solve_round(5, stat, u, uo, meta, (c0,), i, j)
    for f in range(2):
        flat = u[f, PAD + 128 : PAD + 256, :].T
        for z in range(8):
            nat[f, z] = flat[z * 16 + 4 : z * 16 + 12, :]
    for f in range(2, nat.shape[0]):
        nat[f] = jnp.zeros((8, 8, 128), F32)


def coarse_kernel(nat, own, fin, rows):
    i, j = block_here()
    sub = iota((8, 128), 0)
    lane = iota((8, 128), 1)
    tiles = [nat[f, z] for f in range(2) for z in range(8)]
    cols = edge_columns(tiles)
    sums = [jnp.zeros((8, 128), F32) for _ in range(10)]
    left = cols * roll(fin[0], -16, 1)
    right = cols * roll(fin[1], 16, 1)
    for f in range(2):
        acc = jnp.zeros((8, 128), F32)
        for z in range(8):
            c, other = tiles[f * 8 + z], tiles[(1 - f) * 8 + z]
            near = jnp.where(sub == 0, 0.0, roll(c, 1, 0)) + jnp.where(sub == 7, 0.0, roll(c, -1, 0))
            near = near + jnp.where(lane == 0, 0.0, roll(c, 1, 1)) + jnp.where(lane == 127, 0.0, roll(c, -1, 1))
            if z > 0:
                near = near + tiles[f * 8 + z - 1]
            if z < 7:
                near = near + tiles[f * 8 + z + 1]
            s12 = 0.25 * (own[16 + z] - 0.125)
            rhs = (own[40 + z] == f + 1.0).astype(F32) + own[24 + f * 8 + z]
            acc = acc + own[49 + f * 8 + z] * (rhs - ((own[f * 8 + z] + 6.0) * c + s12 * other - near))
        sums[f] = acc
        top = jnp.zeros((8, 128), F32)
        bot = jnp.zeros((8, 128), F32)
        for z in range(8):
            top = jnp.where(sub == z, jnp.broadcast_to(tiles[f * 8 + z][0:1, :], (8, 128)), top)
            bot = jnp.where(sub == z, jnp.broadcast_to(tiles[f * 8 + z][7:8, :], (8, 128)), bot)
        sums[2 + f] = top * fin[2 + f]
        sums[4 + f] = bot * fin[4 + f]
        sums[6 + f] = jnp.where((lane >= f * 8) & (lane < f * 8 + 8), left, 0.0)
        sums[8 + f] = jnp.where((lane >= 16 + f * 8) & (lane < 24 + f * 8), right, 0.0)
    here = i * NGY + j
    slot = iota((2, 128), 0) * 128 + iota((2, 128), 1)
    row = jnp.zeros((2, 128), F32)
    for n, at in enumerate((here, here - NGY, here + NGY, here - 1, here + 1)):
        for f in range(2):
            total = jnp.sum(sums[2 * n + f], keepdims=True) * (1.0 / 8192.0)
            row = jnp.where(slot == 2 * at + f, total, row)
    rows[...] = jnp.broadcast_to(row[None], (NGX * NGY, 2, 128))


def lift_kernel(got, inv, basis, nat, out, coarse):
    q = jnp.sum(got[...], axis=0)
    lane = iota((1, 2), 1)
    pair = jnp.zeros((1, 2), F32)
    for f in range(2):
        c = jnp.sum(q[0:1, :] * inv[0, 0, f : f + 1, 0:128] + q[1:2, :] * inv[0, 0, f : f + 1, 128:256], keepdims=True)
        out[f] = nat[f] + basis[f] * c.reshape(1, 1, 1)
        pair = jnp.where(lane == f, c, pair)
    coarse[0] = pair


def sds(*shape):
    return jax.ShapeDtypeStruct(shape, F32)


def call(kernel, out, scratch=(), **kw):
    return pl.pallas_call(
        kernel,
        out_shape=out,
        scratch_shapes=list(scratch),
        compiler_params=pltpu.CompilerParams(vmem_limit_bytes=48 * 1024 * 1024),
        **kw,
    )


def swap(x, odd):
    return send(x, lambda i, j: (home(i, j), home((((i + odd) ^ 1) - odd) % NGX, j)))


def shards(mixing, forcing, labels, colours, coarse_basis, coarse_inverse):
    coef = lambda t: pltpu.VMEM((6, t, 8, 128), F32)
    block, full = call(
        pack_kernel,
        (sds(49, 8, 128), sds(65, 8, 128)),
        [
            pltpu.VMEM((8, 8, 128), jnp.int32),
            pltpu.SemaphoreType.DMA((8,)),
        ],
        in_specs=[pl.BlockSpec(memory_space=pltpu.HBM)] * 4 + [pl.BlockSpec(memory_space=pltpu.VMEM)],
        name="pack",
    )(
        *(pltpu.with_memory_space_constraint(x, pltpu.HBM) for x in (mixing, forcing, labels, coarse_basis)),
        jnp.broadcast_to(colours, (8, 128)),
    )
    own = send(full, lambda i, j: (i * NGY + j, home(i, j)))
    left = send(block, lambda i, j: (i * NGY + j, home(i, (j + 1) % NGY)))
    right = send(block, lambda i, j: (i * NGY + j, home(i, (j - 1) % NGY)))
    one, two = call(rows_kernel, (sds(27, 8, 384), sds(27, 8, 384)), name="rows")(own, left, right)
    one, two = swap(one, 0), swap(two, 1)
    msg = lambda r: sds(8 * len(message_items(r)), 128)
    stat, u, meta, fin, one, two = call(
        start_kernel,
        (sds(5, ROWS, 128), sds(2, ROWS, 128), sds(24, 128), sds(6, 8, 128), msg(0), msg(0)),
        [pltpu.VMEM((2, 27, 8, 384), F32), pltpu.VMEM((2, 128, 128), F32), pltpu.VMEM((2, ROWS, 128), F32)]
        + [coef(17), coef(16), coef(16)],
        name="round0",
    )(own, left, right, one, two)
    for rnd in range(1, 5):
        one, two = swap(one, 0), swap(two, 1)
        u, one, two = call(
            lambda *refs, rnd=rnd: middle_kernel(rnd, *refs),
            (sds(2, ROWS, 128), msg(rnd), msg(rnd)),
            [pltpu.VMEM((2, ROWS, 128), F32), coef(17), coef(16), coef(16)],
            name=f"round{rnd}",
        )(stat, u, meta, one, two)
    one, two = swap(one, 0), swap(two, 1)
    nat = call(
        last_kernel,
        sds(4, 8, 8, 128),
        [pltpu.VMEM((2, ROWS, 128), F32), pltpu.VMEM((2, ROWS, 128), F32), coef(17)],
        name="round5",
    )(stat, u, meta, one, two)
    back = send(nat, lambda i, j: (home(i, j), i * NGY + j))
    rows = call(coarse_kernel, sds(NGX * NGY, 2, 128), name="coarse")(nat, own, fin)
    got = lax.all_to_all(rows, ("gx", "gy"), 0, 0, tiled=True)
    return call(lift_kernel, (sds(2, 8, 8, 128), sds(1, 1, 2)), name="lift")(got, coarse_inverse, coarse_basis, back)


def solution(mesh):
    return jax.shard_map(
        shards,
        mesh=mesh,
        in_specs=(
            P(None, None, "gx", "gy"),
            P(None, None, "gx", "gy"),
            P(None, "gx", "gy"),
            P("gx", "gy"),
            P(None, None, "gx", "gy"),
            P("gx", "gy", None, None),
        ),
        out_specs=(P(None, None, "gx", "gy"), P("gx", "gy", None)),
        check_vma=False,
    )
```

```python
import jax
import jax.numpy as jnp
from jax import lax
from jax.experimental import pallas as pl
from jax.experimental.pallas import tpu as pltpu
from jax.sharding import PartitionSpec as P

SWEEPS = 20
OMEGA = 0.8
UNROLL = 19
PAD = 8
WIN = (16, 13, 10, 7, 4)
KEEP = (104, 80, 56, 32, 8)
ROWS = 400
F32 = jnp.float32
NGX = 16
NGY = 8


def home(i, j):
    pair, core = i // 2, i % 2
    y, low = (pair, 0) if pair < 4 else (7 - pair, 1)
    return (y * 4 + j // 4 * 2 + core) * NGY + low * 4 + j % 4


def block_here():
    gx, gy = lax.axis_index("gx"), lax.axis_index("gy")
    y, low = gx // 4, gy // 4
    pair = jnp.where(low == 0, y, 7 - y)
    return pair * 2 + gx % 2, gx // 2 % 2 * 4 + gy % 4


def send(x, to):
    blocks = [(i, j) for i in range(NGX) for j in range(NGY)]
    return lax.ppermute(x, ("gx", "gy"), [to(i, j) for i, j in blocks])


def iota(shape, dim):
    return lax.broadcasted_iota(jnp.int32, shape, dim)


def roll(x, by, axis):
    by = by % x.shape[axis]
    return x if by == 0 else pltpu.roll(x, by, axis)


def lane_ids():
    lane = iota((8, 128), 1)
    return lane & 15, lane >> 4


def edge_columns(tiles):
    lane = iota((8, 128), 1)
    out = jnp.zeros((8, 128), F32)
    for n, tile in enumerate(tiles):
        out = jnp.where(lane == n, roll(tile, n, 1), out)
        out = jnp.where(lane == 16 + n, roll(tile, 17 + n, 1), out)
    return out


def pack_kernel(mix, forc, lab, basis, colour, out, full, lab_v, sems):
    copies = [
        pltpu.make_async_copy(lab, lab_v, sems.at[0]),
        pltpu.make_async_copy(basis.at[0], full.at[pl.ds(49, 8)], sems.at[1]),
        pltpu.make_async_copy(basis.at[1], full.at[pl.ds(57, 8)], sems.at[2]),
    ]
    for f in range(3):
        copies.append(pltpu.make_async_copy(mix.at[f], out.at[pl.ds(f * 8, 8)], sems.at[3 + f]))
    for f in range(2):
        copies.append(pltpu.make_async_copy(forc.at[f], out.at[pl.ds(24 + f * 8, 8)], sems.at[6 + f]))
    for c in copies:
        c.start()
    for c in copies:
        c.wait()
    out[40:48] = lab_v[...].astype(F32)
    cols = edge_columns([full[49 + n] for n in range(16)])
    lane = iota((8, 128), 1)
    out[48] = jnp.where(lane == 32, colour[...].astype(F32), cols)
    full[0:49] = out[...]


def rows_kernel(own, left, right, first, second):
    even = block_here()[0] % 2 == 0
    pl.when(even)(lambda: write_rows(own, left, right, second, first))
    pl.when(jnp.logical_not(even))(lambda: write_rows(own, left, right, first, second))


def write_rows(own, left, right, up, down):
    for part, ref in enumerate((left, own, right)):
        lanes = slice(part * 128, part * 128 + 128)
        for a in range(6):
            for p in range(4):
                lo, hi = ref[a * 8 + 2 * p], ref[a * 8 + 2 * p + 1]
                sub = iota((8, 128), 0)
                up[a * 4 + p, :, lanes] = jnp.where(sub < 4, lo, roll(hi, 4, 0))
                down[a * 4 + p, :, lanes] = jnp.where(sub < 4, roll(lo, 4, 0), hi)
        for z in range(8):
            up[24, z : z + 1, lanes] = ref[40 + z, 4:5, :]
            down[24, z : z + 1, lanes] = ref[40 + z, 3:4, :]
            for f in range(2):
                if part == 1:
                    up[25 + f, z : z + 1, lanes] = own[49 + f * 8 + z, 0:1, :]
                    down[25 + f, z : z + 1, lanes] = own[49 + f * 8 + z, 7:8, :]
        if part != 1:
            up[25:27, :, lanes] = jnp.zeros((2, 8, 128), F32)
            down[25:27, :, lanes] = jnp.zeros((2, 8, 128), F32)


def window_rows(kind, tiles):
    if kind == 0:
        return PAD + 128 - 4
    if kind == 1:
        return PAD + 128 + 4 - 8 * tiles
    return PAD + 128 + 124


def prepare(kind, tiles, stat, u, uo, coef, i, j):
    row0 = window_rows(kind, tiles)
    xp, z = lane_ids()
    sub = iota((8, 128), 0)
    rim_x = ((xp == 0) | (xp == 15)).astype(F32)
    gx = i * 8 + xp - 4
    in_x = ((gx >= 0) & (gx < NGX * 8)).astype(F32)
    for t in range(tiles):
        at = pl.ds(row0 + t, 8, stride=tiles)
        s11, s22, s12 = stat[0, at, :], stat[1, at, :], stat[2, at, :]
        y = row0 - PAD - 128 + sub * tiles + t + j * 128
        inside = in_x * ((y >= 0) & (y < NGY * 128)).astype(F32)
        diag = 6.0 + rim_x
        if t == 0 and kind != 1:
            diag = diag + (sub == 0).astype(F32)
        if t == tiles - 1 and kind != 2:
            diag = diag + (sub == 7).astype(F32)
        vals = []
        for f in range(2):
            c = u[f, at, :]
            near = u[f, pl.ds(row0 + t - 1, 8, stride=tiles), :] + u[f, pl.ds(row0 + t + 1, 8, stride=tiles), :]
            out = uo[f, at, :]
            near = near + jnp.where(xp == 0, out, roll(c, 1, 1)) + jnp.where(xp == 15, out, roll(c, -1, 1))
            near = near + jnp.where(z == 0, 0.0, roll(c, 16, 1)) + jnp.where(z == 7, 0.0, roll(c, -16, 1))
            vals.append((c, near))
        for f, s in ((0, s11), (1, s22)):
            c, near = vals[f]
            r = stat[3 + f, at, :] - ((s + 6.0) * c + s12 * vals[1 - f][0] - near)
            w = OMEGA * inside / (s + diag)
            coef[f, t] = w
            coef[2 + f, t] = w * s12
            coef[4 + f, t] = w * r


def adjacency():
    a, b = iota((128, 128), 0), iota((128, 128), 1)
    ax, az, bx, bz = a & 15, a >> 4, b & 15, b >> 4
    near_x = (az == bz) & ((ax - bx == 1) | (bx - ax == 1))
    near_z = (ax == bx) & ((az - bz == 1) | (bz - az == 1))
    one = (near_x | near_z).astype(F32).astype(jnp.bfloat16)
    return jnp.concatenate([one, one], 0)


def sweep(e, tiles, coef, adj):
    sub = iota((8, 128), 0)
    flat = jnp.concatenate(e[0] + e[1], 0)
    hi = flat.astype(jnp.bfloat16)
    lo = (flat - hi.astype(F32)).astype(jnp.bfloat16)
    side = jnp.dot(jnp.concatenate([hi, lo], 1), adj, preferred_element_type=F32)
    new = [[], []]
    for f in range(2):
        for t in range(tiles):
            c = e[f][t]
            before = e[f][t - 1] if t else jnp.where(sub == 0, 0.0, roll(e[f][tiles - 1], 1, 0))
            after = e[f][t + 1] if t + 1 < tiles else jnp.where(sub == 7, 0.0, roll(e[f][0], -1, 0))
            at = (f * tiles + t) * 8
            near = before + after + side[at : at + 8]
            new[f].append((1.0 - OMEGA) * c + coef[4 + f, t] + (coef[f, t] * near - coef[2 + f, t] * e[1 - f][t]))
    return new


def sweeps(kind, tiles, u, coef):
    row0 = window_rows(kind, tiles)
    xp, z = lane_ids()
    sub = iota((8, 128), 0)
    adj = adjacency()

    def body(_, flat):
        e = [list(flat[:tiles]), list(flat[tiles:])]
        for _ in range(UNROLL):
            e = sweep(e, tiles, coef, adj)
        return tuple(e[0] + e[1])

    flat = tuple(coef[4 + f, t] for f in range(2) for t in range(tiles))
    for _ in range((SWEEPS - 1) % UNROLL):
        e = sweep([list(flat[:tiles]), list(flat[tiles:])], tiles, coef, adj)
        flat = tuple(e[0] + e[1])
    if SWEEPS - 1 == UNROLL:
        flat = body(0, flat)
    else:
        flat = lax.fori_loop(0, (SWEEPS - 1) // UNROLL, body, flat)
    own_x = (xp >= 4) & (xp < 12)
    for t in range(tiles):
        at = pl.ds(row0 + t, 8, stride=tiles)
        y = row0 - PAD - 128 + sub * tiles + t
        if kind == 0:
            here = own_x & (y >= 0) & (y < 128)
        elif kind == 1:
            here = own_x & (y < 0)
        else:
            here = own_x & (y >= 128)
        for f in range(2):
            u[f, at, :] = u[f, at, :] + jnp.where(here, flat[f * tiles + t], 0.0)


def solve_round(rnd, stat, u, uo, meta, coefs, i, j):
    own = jnp.max(meta[0:8, :])
    left = jnp.max(meta[8:16, :])
    right = jnp.max(meta[16:24, :])
    jobs = [(0, 17, own, coefs[0])]
    if rnd < 5:
        jobs += [(1, WIN[rnd], left, coefs[1]), (2, WIN[rnd], right, coefs[2])]
    for kind, tiles, colour, coef in jobs:
        pl.when(colour == float(rnd))(lambda kind=kind, tiles=tiles, coef=coef: prepare(kind, tiles, stat, u, uo, coef, i, j))
    for kind, tiles, colour, coef in jobs:
        pl.when(colour == float(rnd))(lambda kind=kind, tiles=tiles, coef=coef: sweeps(kind, tiles, u, coef))


def message_items(rnd):
    tiles = (128 + 2 * KEEP[rnd]) // 8
    items = [(f, PAD + 128 - KEEP[rnd] + 8 * q) for f in range(2) for q in range(tiles)]
    third = len(items) // 3
    return [[items[g * third + m] for g in range(3)] for m in range(third)]


def emit(rnd, u, first, second, even):
    xp, _ = lane_ids()

    def write(up, down):
        for m, trio in enumerate(message_items(rnd)):
            tiles = [u[f, pl.ds(row, 8), :] for f, row in trio]
            at = pl.ds(8 * m, 8)
            for ref, lane0 in ((up, 4), (down, 7)):
                a, b, c = (roll(tile, 5 * g - lane0, 1) for g, tile in enumerate(tiles))
                ref[at, :] = jnp.where(xp < 5, a, jnp.where(xp < 10, b, c))

    pl.when(even)(lambda: write(second, first))
    pl.when(jnp.logical_not(even))(lambda: write(first, second))


def absorb(rnd, u, uo, first, second, i):
    xp, _ = lane_ids()
    has_above = (i > 0).astype(F32)
    has_below = (i < NGX - 1).astype(F32)

    def read(above, below):
        for m, trio in enumerate(message_items(rnd)):
            a = above[pl.ds(8 * m, 8), :] * has_above
            b = below[pl.ds(8 * m, 8), :] * has_below
            for g, (f, row) in enumerate(trio):
                at = pl.ds(row, 8)
                inner = jnp.where(xp >= 12, roll(b, 12 - 5 * g, 1), u[f, at, :])
                u[f, at, :] = jnp.where(xp < 4, roll(a, -5 * g - 1, 1), inner)
                uo[f, at, :] = jnp.where(xp == 0, roll(a, -5 * g, 1), roll(b, 11 - 5 * g, 1))

    even = i % 2 == 0
    pl.when(even)(lambda: read(second, first))
    pl.when(jnp.logical_not(even))(lambda: read(first, second))


def start_kernel(own, left, right, first, second, stat, u, meta, fin, out1, out2, near, buf, uo, c0, c1, c2):
    i, j = block_here()
    even = i % 2 == 0

    def place(above, below):
        near[0] = above[...]
        near[1] = below[...]

    pl.when(even)(lambda: place(second, first))
    pl.when(jnp.logical_not(even))(lambda: place(first, second))
    above, below = near.at[0], near.at[1]
    xp, _ = lane_ids()
    lane = iota((8, 128), 1)
    full_lane = iota((128, 128), 1)
    full_xp = full_lane & 15
    gx = i * 8 + full_xp - 4
    in_x = (gx >= 0) & (gx < NGX * 8)
    for n, ref in enumerate((own, left, right)):
        valid = ((j > 0) if n == 1 else (j < NGY - 1)) if n else (j >= 0)
        colour = jnp.where(lane == 32, jnp.where(valid, 1.0, 0.0) * (ref[48] + 1.0), 0.0) - 1.0
        meta[n * 8 : n * 8 + 8, :] = colour
    fin[0] = left[48] * (j > 0).astype(F32)
    fin[1] = right[48] * (j < NGY - 1).astype(F32)
    for f in range(2):
        fin[2 + f] = above[25 + f, :, 128:256] * (i > 0).astype(F32)
        fin[4 + f] = below[25 + f, :, 128:256] * (i < NGX - 1).astype(F32)
    for f in range(2):
        u[f, 0:PAD, :] = jnp.zeros((PAD, 128), F32)
        u[f, ROWS - PAD : ROWS, :] = jnp.zeros((PAD, 128), F32)
    for part, ref in enumerate((left, own, right)):
        lanes = slice(part * 128, part * 128 + 128)
        rows = slice(PAD + part * 128, PAD + part * 128 + 128)
        gy = (j - 1 + part) * 128
        in_y = (gy >= 0) & (gy < NGY * 128)

        def gather(a):
            slot = a % 2
            for p in range(4):
                for h in range(2):
                    z = 2 * p + h
                    buf[slot, z * 16 : z * 16 + 4, :] = above[a * 4 + p, 4 * h : 4 * h + 4, lanes]
                    buf[slot, z * 16 + 4 : z * 16 + 12, :] = ref[a * 8 + z]
                    buf[slot, z * 16 + 12 : z * 16 + 16, :] = below[a * 4 + p, 4 * h : 4 * h + 4, lanes]
            return buf[slot].T

        stat[0, rows, :] = gather(0)
        stat[1, rows, :] = gather(1)
        stat[2, rows, :] = 0.25 * (gather(2) - 0.125)
        force = [gather(3), gather(4)]
        label = gather(5)
        buf[0] = jnp.zeros((128, 128), F32)
        for z in range(8):
            buf[0, z * 16 : z * 16 + 1, :] = above[24, z : z + 1, lanes]
            buf[0, z * 16 + 15 : z * 16 + 16, :] = below[24, z : z + 1, lanes]
        outer = buf[0].T
        y_ok = in_y.astype(F32)
        out_ok = jnp.where(full_xp == 0, (i > 0).astype(F32), (i < NGX - 1).astype(F32)) * y_ok
        for f in range(2):
            hot = (label == f + 1.0).astype(F32) * (in_x.astype(F32) * y_ok)
            u[f, rows, :] = hot
            stat[3 + f, rows, :] = hot + force[f]
            uo[f, rows, :] = (outer == f + 1.0).astype(F32) * out_ok
    solve_round(0, stat, u, uo, meta, (c0, c1, c2), i, j)
    emit(0, u, out1, out2, even)


def middle_kernel(rnd, stat, u_in, meta, first, second, u, out1, out2, uo, c0, c1, c2):
    i, j = block_here()
    u[...] = u_in[...]
    absorb(rnd - 1, u, uo, first, second, i)
    solve_round(rnd, stat, u, uo, meta, (c0, c1, c2), i, j)
    emit(rnd, u, out1, out2, i % 2 == 0)


def last_kernel(stat, u_in, meta, first, second, nat, u, uo, c0):
    i, j = block_here()
    u[...] = u_in[...]
    absorb(4, u, uo, first, second, i)
    solve_round(5, stat, u, uo, meta, (c0,), i, j)
    for f in range(2):
        flat = u[f, PAD + 128 : PAD + 256, :].T
        for z in range(8):
            nat[f, z] = flat[z * 16 + 4 : z * 16 + 12, :]


def coarse_kernel(nat, own, fin, rows):
    i, j = block_here()
    sub = iota((8, 128), 0)
    lane = iota((8, 128), 1)
    tiles = [nat[f, z] for f in range(2) for z in range(8)]
    cols = edge_columns(tiles)
    sums = [jnp.zeros((8, 128), F32) for _ in range(10)]
    left = cols * roll(fin[0], -16, 1)
    right = cols * roll(fin[1], 16, 1)
    for f in range(2):
        acc = jnp.zeros((8, 128), F32)
        for z in range(8):
            c, other = tiles[f * 8 + z], tiles[(1 - f) * 8 + z]
            near = jnp.where(sub == 0, 0.0, roll(c, 1, 0)) + jnp.where(sub == 7, 0.0, roll(c, -1, 0))
            near = near + jnp.where(lane == 0, 0.0, roll(c, 1, 1)) + jnp.where(lane == 127, 0.0, roll(c, -1, 1))
            if z > 0:
                near = near + tiles[f * 8 + z - 1]
            if z < 7:
                near = near + tiles[f * 8 + z + 1]
            s12 = 0.25 * (own[16 + z] - 0.125)
            rhs = (own[40 + z] == f + 1.0).astype(F32) + own[24 + f * 8 + z]
            acc = acc + own[49 + f * 8 + z] * (rhs - ((own[f * 8 + z] + 6.0) * c + s12 * other - near))
        sums[f] = acc
        top = jnp.zeros((8, 128), F32)
        bot = jnp.zeros((8, 128), F32)
        for z in range(8):
            top = jnp.where(sub == z, jnp.broadcast_to(tiles[f * 8 + z][0:1, :], (8, 128)), top)
            bot = jnp.where(sub == z, jnp.broadcast_to(tiles[f * 8 + z][7:8, :], (8, 128)), bot)
        sums[2 + f] = top * fin[2 + f]
        sums[4 + f] = bot * fin[4 + f]
        sums[6 + f] = jnp.where((lane >= f * 8) & (lane < f * 8 + 8), left, 0.0)
        sums[8 + f] = jnp.where((lane >= 16 + f * 8) & (lane < 24 + f * 8), right, 0.0)
    here = i * NGY + j
    slot = iota((2, 128), 0) * 128 + iota((2, 128), 1)
    row = jnp.zeros((2, 128), F32)
    for n, at in enumerate((here, here - NGY, here + NGY, here - 1, here + 1)):
        for f in range(2):
            total = jnp.sum(sums[2 * n + f], keepdims=True) * (1.0 / 8192.0)
            row = jnp.where(slot == 2 * at + f, total, row)
    rows[...] = jnp.broadcast_to(row[None], (NGX * NGY, 2, 128))


def lift_kernel(got, inv, basis, nat, out, coarse):
    q = jnp.sum(got[...], axis=0)
    lane = iota((1, 2), 1)
    pair = jnp.zeros((1, 2), F32)
    for f in range(2):
        c = jnp.sum(q[0:1, :] * inv[0, 0, f : f + 1, 0:128] + q[1:2, :] * inv[0, 0, f : f + 1, 128:256], keepdims=True)
        out[f] = nat[f] + basis[f] * c.reshape(1, 1, 1)
        pair = jnp.where(lane == f, c, pair)
    coarse[0] = pair


def sds(*shape):
    return jax.ShapeDtypeStruct(shape, F32)


def call(kernel, out, scratch=(), **kw):
    return pl.pallas_call(
        kernel,
        out_shape=out,
        scratch_shapes=list(scratch),
        compiler_params=pltpu.CompilerParams(vmem_limit_bytes=48 * 1024 * 1024),
        **kw,
    )


def swap(x, odd):
    return send(x, lambda i, j: (home(i, j), home((((i + odd) ^ 1) - odd) % NGX, j)))


def shards(mixing, forcing, labels, colours, coarse_basis, coarse_inverse):
    coef = lambda t: pltpu.VMEM((6, t, 8, 128), F32)
    block, full = call(
        pack_kernel,
        (sds(49, 8, 128), sds(65, 8, 128)),
        [
            pltpu.VMEM((8, 8, 128), jnp.int32),
            pltpu.SemaphoreType.DMA((8,)),
        ],
        in_specs=[pl.BlockSpec(memory_space=pltpu.HBM)] * 4 + [pl.BlockSpec(memory_space=pltpu.VMEM)],
        name="pack",
    )(
        *(pltpu.with_memory_space_constraint(x, pltpu.HBM) for x in (mixing, forcing, labels, coarse_basis)),
        jnp.broadcast_to(colours, (8, 128)),
    )
    own = send(full, lambda i, j: (i * NGY + j, home(i, j)))
    left = send(block, lambda i, j: (i * NGY + j, home(i, (j + 1) % NGY)))
    right = send(block, lambda i, j: (i * NGY + j, home(i, (j - 1) % NGY)))
    one, two = call(rows_kernel, (sds(27, 8, 384), sds(27, 8, 384)), name="rows")(own, left, right)
    one, two = swap(one, 0), swap(two, 1)
    msg = lambda r: sds(8 * len(message_items(r)), 128)
    stat, u, meta, fin, one, two = call(
        start_kernel,
        (sds(5, ROWS, 128), sds(2, ROWS, 128), sds(24, 128), sds(6, 8, 128), msg(0), msg(0)),
        [pltpu.VMEM((2, 27, 8, 384), F32), pltpu.VMEM((2, 128, 128), F32), pltpu.VMEM((2, ROWS, 128), F32)]
        + [coef(17), coef(16), coef(16)],
        name="round0",
    )(own, left, right, one, two)
    for rnd in range(1, 5):
        one, two = swap(one, 0), swap(two, 1)
        u, one, two = call(
            lambda *refs, rnd=rnd: middle_kernel(rnd, *refs),
            (sds(2, ROWS, 128), msg(rnd), msg(rnd)),
            [pltpu.VMEM((2, ROWS, 128), F32), coef(17), coef(16), coef(16)],
            name=f"round{rnd}",
        )(stat, u, meta, one, two)
    one, two = swap(one, 0), swap(two, 1)
    nat = call(
        last_kernel,
        sds(2, 8, 8, 128),
        [pltpu.VMEM((2, ROWS, 128), F32), pltpu.VMEM((2, ROWS, 128), F32), coef(17)],
        name="round5",
    )(stat, u, meta, one, two)
    back = send(nat, lambda i, j: (home(i, j), i * NGY + j))
    rows = call(coarse_kernel, sds(NGX * NGY, 2, 128), name="coarse")(nat, own, fin)
    got = lax.all_to_all(rows, ("gx", "gy"), 0, 0, tiled=True)
    return call(lift_kernel, (sds(2, 8, 8, 128), sds(1, 1, 2)), name="lift")(got, coarse_inverse, coarse_basis, back)


def solution(mesh):
    return jax.shard_map(
        shards,
        mesh=mesh,
        in_specs=(
            P(None, None, "gx", "gy"),
            P(None, None, "gx", "gy"),
            P(None, "gx", "gy"),
            P("gx", "gy"),
            P(None, None, "gx", "gy"),
            P("gx", "gy", None, None),
        ),
        out_specs=(P(None, None, "gx", "gy"), P("gx", "gy", None)),
        check_vma=False,
    )
```
